256 devices in a mesh: rep: 8 (over y, core), shard: 32 (over z, x).
Axes of the slice: x: 4, y: 4, z: 8, core: 2. Of those that a mesh axis runs over, the one named last changes fastest.
Arguments:
- grad_kv: bfloat16 [8, 2, 8192, 1024], P('rep', None, 'shard'), may hold values from -24 to 24
- error_kv: float32 [8, 2, 8192, 1024], P('rep', None, 'shard'), may hold values from -12 to 12
- basis_kv: float32 [2, 1024, 64], replicated, may hold values from -6 to 6
Outputs:
- update_kv: bfloat16 [2, 8192, 1024], P(None, 'shard')
- new_error: float32 [8, 2, 8192, 1024], P('rep', None, 'shard')
- basis_next: float32 [2, 1024, 64], replicated
The draws below stay inside these ranges and needn't reach their ends.
All inputs are finite; a program needn't handle non-finite values.
Results may differ from the reference program's by a relative error of at most 0.001.
Values sent between devices are 32-bit elements; how exact they have to be, the bound alone decides.
A program may use at most 64 MiB of HBM per device.

```python
import jax
import jax.numpy as jnp
from jax import lax

D = 8192
RANK = 64
KVC = 1024
REPLICAS = 8
N_REP = 8


def block_levels(rng, shape, pieces, least, high):
    gain = 1.0
    for position, shards_of in pieces:
        steps = jax.random.uniform(jax.random.fold_in(jax.random.fold_in(rng, 6), position), (shards_of,), jnp.float32, least / len(pieces), high / len(pieces))
        gain = gain * jnp.repeat(jnp.exp(steps), shape[position] // shards_of).reshape((-1,) + (1,) * (len(shape) - 1 - position))
    return gain


def centred(rng, shape, deviation, bound, cuts=(), kind=jnp.bfloat16):
    loudness = block_levels(rng, shape, cuts, -0.22, 0.18) if cuts else 1.0
    array = jax.random.normal(rng, shape, jnp.float32) * deviation * loudness
    return jnp.minimum(jnp.maximum(array, -bound), bound).astype(kind)


def setup_inputs(seed: int = 0) -> dict:
    keys = jax.random.split(jax.random.key(seed), 4)
    return {
        "grad_kv": centred(keys[0], (REPLICAS, 2, D, KVC), 4.0, 24.0, ((0, 8), (2, 32))),
        "error_kv": centred(keys[1], (REPLICAS, 2, D, KVC), 2.0, 12.0, ((0, 8), (2, 32)), jnp.float32),
        "basis_kv": centred(keys[2], (2, KVC, RANK), 1.0, 6.0, (), jnp.float32),
    }


def reference(grad_kv, error_kv, basis_kv):
    highest = lax.Precision.HIGHEST
    merged = grad_kv.astype(jnp.float32) + error_kv
    left = jnp.einsum('smrc,mck->mrk', merged, basis_kv, precision=highest) / N_REP
    gram = jnp.einsum('mrk,mrl->mkl', left, left, precision=highest)
    chol = jnp.linalg.cholesky(gram)
    ortho = lax.linalg.triangular_solve(chol, left, left_side=False, lower=True, transpose_a=True)
    basis_next = jnp.einsum('smrc,mrk->mck', merged, ortho, precision=highest) / N_REP
    approx = jnp.einsum('mrk,mck->mrc', ortho, basis_next, precision=highest)
    new_error = merged - approx[None]
    return (approx.astype(jnp.bfloat16), new_error, basis_next)
```

```python
import functools

import jax
import jax.numpy as jnp
from jax import lax
from jax.experimental import pallas as pl
from jax.experimental.pallas import tpu as pltpu
from jax.sharding import PartitionSpec as P

MESH = pl.DeviceIdType.MESH
F32 = jnp.float32
BF16 = jnp.bfloat16
HIGHEST = lax.Precision.HIGHEST

ROWS = 256
KVC = 1024
RANK = 64
NX, NY, NZ = 4, 4, 8
NQ = 4
QR = ROWS // NQ
NCH = 2
CW = KVC // NCH
PW = CW // 2
PLANE = [(dx, dy) for dx in range(NX) for dy in range(NY) if dx or dy]


def split(x):
    hi = x.astype(BF16)
    return hi, (x - hi.astype(F32)).astype(BF16)


def nt(a, b, **kw):
    return lax.dot_general(a, b, (((1,), (1,)), ((), ())), preferred_element_type=F32, **kw)


def nn(a, b, **kw):
    return lax.dot_general(a, b, (((1,), (0,)), ((), ())), preferred_element_type=F32, **kw)


def factor_panels(blocks, panels):
    sub_i = lax.broadcasted_iota(jnp.int32, (8, 128), 0)
    for kb in panels:
        live = range(kb, 8)
        cols = {
            b: [jnp.broadcast_to(blocks[b][:, 8 * kb + j : 8 * kb + j + 1], (8, 128)) for j in range(8)]
            for b in live
        }
        for s in range(8):
            row = jnp.broadcast_to(blocks[kb][s : s + 1, :], (8, 128))
            inv = 1.0 / jnp.broadcast_to(cols[kb][s][s : s + 1, :], (8, 128))
            heads = [jnp.broadcast_to(cols[kb][j][s : s + 1, :], (8, 128)) for j in range(8)]
            for b in live:
                f = cols[b][s] * inv
                if b == kb:
                    f = jnp.where(sub_i > s, f, 0.0)
                blocks[b] = blocks[b] - f * row
                for j in range(s + 1, 8):
                    cols[b][j] = cols[b][j] - f * heads[j]
    return blocks


def comm_kernel(
    grad_ref, err_ref, basis_ref,
    rt_out, cinv_out, ot_out,
    g_o, e_o, g_s, e_s, b_v, mo, pin, p_hi, p_lo,
    l1, lr1, l2, lr2,
    gz_b, gz_r, gx_b, gx_r,
    rs_b, rs_r, z_b, z_r, ag_b, w_b,
    ld, px_s, px_r, l_s, l_r, g_ss, g_rs, rs_s, rs_rs, z_s, z_rs, ag_s, ag_rs, fw_s, fw_r, co_s, co_r,
):
    rep, shard = lax.axis_index("rep"), lax.axis_index("shard")
    y, c = rep // 2, rep % 2
    z, x = shard // NX, shard % NX

    def dev(yy, zz, xx, cc=None):
        return (yy * 2 + (c if cc is None else cc), zz * NX + xx)

    partner = dev(y, z, x, 1 - c)
    plane = [(dx, dy, dev((y + dy) % NY, z, (x + dx) % NX)) for dx, dy in PLANE]
    zline = [dev(y, (z + d) % NZ, x) for d in range(1, NZ)]
    xline = [dev(y, z, (x + d) % NX) for d in range(1, NX)]

    def remote(src, dst, ss, rs, to):
        copy = pltpu.make_async_remote_copy(
            src_ref=src, dst_ref=dst, send_sem=ss, recv_sem=rs, device_id=to, device_id_type=MESH
        )
        copy.start()
        return copy

    def wait_bytes(ref, sem):
        pltpu.make_async_copy(ref, ref, sem).wait()

    oc = 1 - c
    loads = []
    for q in range(NQ):
        rows = pl.ds(q * QR, QR)
        pair = []
        for k, (hbm, buf) in enumerate(((grad_ref, g_o), (err_ref, e_o))):
            cp = pltpu.make_async_copy(hbm.at[oc, rows, :], buf.at[rows, :], ld.at[2 * q + k])
            cp.start()
            pair.append(cp)
        loads.append(pair)
    own_b = pltpu.make_async_copy(basis_ref.at[c], b_v, ld.at[2 * NQ])
    own_b.start()
    own_g = pltpu.make_async_copy(grad_ref.at[c], g_s, ld.at[2 * NQ + 1])
    own_g.start()
    own_e = pltpu.make_async_copy(err_ref.at[c], e_s, ld.at[2 * NQ + 2])
    own_e.start()

    barrier = pltpu.get_barrier_semaphore()
    peers = [partner] + [d for _, _, d in plane] + zline
    for d in peers:
        pl.semaphore_signal(barrier, inc=1, device_id=d, device_id_type=MESH)
    pl.semaphore_wait(barrier, len(peers))

    px = []
    for q in range(NQ):
        rows = pl.ds(q * QR, QR)
        loads[q][0].wait()
        loads[q][1].wait()
        mo[q] = g_o[rows, :].astype(F32) + e_o[rows, :]
        px.append(remote(mo.at[q], pin.at[q], px_s.at[q], px_r.at[q], partner))
    own_b.wait()
    bt = b_v[...].T
    bt_h, bt_l = split(bt)
    bt2 = jnp.concatenate([bt_h, bt_l], axis=0)
    own_g.wait()
    own_e.wait()
    for q in range(NQ):
        rows = pl.ds(q * QR, QR)
        px[q].wait_recv()
        p = g_s[rows, :].astype(F32) + e_s[rows, :] + pin[q]
        h, l = split(p)
        p_hi[rows, :] = h
        p_lo[rows, :] = l

    ph = p_hi[...]
    pw = p_lo[...]
    t = nt(bt2, ph)
    lt = (t[:RANK] + t[RANK:] + nt(bt_h, pw)) * 0.125
    l1[...] = lt
    flip = y + 1 - 2 * (y % 2)
    side = (y + 3 + 2 * (y % 2)) % NY
    d_flip, d_side = dev(flip, z, x), dev(side, z, x)
    half = RANK // 2
    lo_half, hi_half = pl.ds(0, half), pl.ds(half, half)
    a1 = remote(l1.at[lo_half], lr1.at[lo_half], l_s.at[0], l_r.at[0], d_flip)
    b1 = remote(l1.at[hi_half], lr1.at[hi_half], l_s.at[1], l_r.at[1], d_side)
    a1.wait_recv()
    l2[lo_half, :] = lt[:half] + lr1[lo_half, :]
    a2 = remote(l2.at[lo_half], lr2.at[lo_half], l_s.at[2], l_r.at[2], d_side)
    b1.wait_recv()
    l2[hi_half, :] = lt[half:] + lr1[hi_half, :]
    b2 = remote(l2.at[hi_half], lr2.at[hi_half], l_s.at[3], l_r.at[3], d_flip)
    a2.wait_recv()
    b2.wait_recv()
    lt = l2[...] + lr2[...]

    gram = nt(lt, lt, precision=HIGHEST)
    gz_b[...] = jnp.concatenate([gram[: RANK // 2], gram[RANK // 2 :]], axis=1)
    gz = [remote(gz_b, gz_r.at[d], g_ss.at[0], g_rs.at[0], to) for d, to in enumerate(zline)]

    lt_h, lt_l = split(lt)
    lt2 = jnp.concatenate([lt_h, lt_l], axis=0)

    def piece(ref, p, j):
        rows = pl.ds(pl.multiple_of((p // 2) * 8, 8), 8)
        cols = pl.ds(pl.multiple_of(j * CW + (p % 2) * PW, PW), PW)
        return rows, cols

    me = y * NX + x
    for j in range(NCH):
        t = nn(lt2, p_hi[:, j * CW : (j + 1) * CW])
        rs_b[:, j * CW : (j + 1) * CW] = t[:RANK] + t[RANK:] + nn(lt_h, p_lo[:, j * CW : (j + 1) * CW])
        for i, (dx, dy, to) in enumerate(plane):
            at = ((y + dy) % NY) * NX + (x + dx) % NX
            rows, cols = piece(rs_b, at, j)
            remote(rs_b.at[rows, cols], rs_r.at[j, i], rs_s.at[j], rs_rs.at[j], to)

    def gram_z():
        wait_bytes(gz_r, g_rs.at[0])
        r = [gz_b[...]] + [gz_r[d] for d in range(NZ - 1)]
        gx_b[...] = ((r[0] + r[4]) + (r[2] + r[6])) + ((r[1] + r[5]) + (r[3] + r[7]))
        for d, to in enumerate(xline):
            remote(gx_b, gx_r.at[d], g_ss.at[1], g_rs.at[1], to)

    def sum_rs(j):
        wait_bytes(rs_r.at[j], rs_rs.at[j])
        rows, cols = piece(rs_b, me, j)
        r = [rs_b[rows, cols]] + [rs_r[j, i] for i in range(len(PLANE))]
        while len(r) > 1:
            r = [r[i] + r[i + 1] for i in range(0, len(r), 2)]
        z_b[j] = r[0]
        for d, to in enumerate(zline):
            remote(z_b.at[j], z_r.at[j, d], z_s.at[j], z_rs.at[j], to)

    def sum_z(j):
        wait_bytes(z_r.at[j], z_rs.at[j])
        r = [z_b[j]] + [z_r[j, d] for d in range(NZ - 1)]
        total = ((r[0] + r[4]) + (r[2] + r[6])) + ((r[1] + r[5]) + (r[3] + r[7]))
        rows, cols = piece(rs_b, me, j)
        ag_b[j] = total
        rt_out[c, rows, cols] = total
        for _, _, to in plane:
            remote(ag_b.at[j], rt_out.at[c, rows, cols], ag_s.at[j], ag_rs.at[j], to)

    sum_rs(0)
    gram_z()
    for j in range(1, NCH):
        sum_rs(j)
    wait_bytes(gx_r, g_rs.at[1])
    g = (gx_b[...] + gx_r[1]) + (gx_r[0] + gx_r[2])
    gram = jnp.concatenate([g[:, :RANK], g[:, RANK:]], axis=0)
    ri = lax.broadcasted_iota(jnp.int32, (RANK, RANK), 0)
    ci = lax.broadcasted_iota(jnp.int32, (RANK, RANK), 1)
    w = jnp.concatenate([gram, jnp.where(ri == ci, 1.0, 0.0)], axis=1)
    blocks = [w[8 * b : 8 * b + 8] for b in range(8)]
    blocks = factor_panels(blocks, range(0, 2))
    for j in range(NCH):
        sum_z(j)
    blocks = factor_panels(blocks, range(2, 8))
    w = jnp.concatenate(blocks, axis=0)
    u, low = w[:, :RANK], w[:, RANK:]
    diag = jnp.sum(jnp.where(ri == ci, u, 0.0), axis=1, keepdims=True)
    cinv = low * lax.rsqrt(diag)
    w_b[...] = jnp.concatenate([cinv, jnp.zeros_like(cinv)], axis=1)
    cinv_out[c] = w_b[...]
    ot_out[c] = nn(cinv, lt, precision=HIGHEST)
    remote(cinv_out.at[c], cinv_out.at[c], co_s.at[0], co_r.at[0], partner)
    remote(ot_out.at[c], ot_out.at[c], co_s.at[1], co_r.at[1], partner)
    for j in range(NCH):
        wait_bytes(rs_r.at[j], ag_rs.at[j])
        cols = pl.ds(j * CW, CW)
        remote(rt_out.at[c, :, cols], rt_out.at[c, :, cols], fw_s.at[j], fw_r.at[j], partner)

    wait_bytes(cinv_out.at[oc], co_r.at[0])
    wait_bytes(ot_out.at[oc], co_r.at[1])
    for j in range(NCH):
        wait_bytes(rt_out.at[oc, :, pl.ds(j * CW, CW)], fw_r.at[j])
    for q in range(NQ):
        px[q].wait_send()
    for cp in (a1, b1, a2, b2):
        cp.wait_send()
    wait_bytes(gz_r, g_ss.at[0])
    wait_bytes(gx_r, g_ss.at[1])
    for j in range(NCH):
        wait_bytes(rs_r.at[j], rs_s.at[j])
        wait_bytes(z_r.at[j], z_s.at[j])
        wait_bytes(rs_r.at[j], ag_s.at[j])
        wait_bytes(rt_out.at[c, :, pl.ds(j * CW, CW)], fw_s.at[j])
    wait_bytes(cinv_out.at[c], co_s.at[0])
    wait_bytes(ot_out.at[c], co_s.at[1])


RB = 128


def out_kernel(grad_ref, err_ref, rt_ref, cinv_ref, ot_ref, upd_ref, new_ref, next_ref, r3, o3):
    i = pl.program_id(1)

    @pl.when(i == 0)
    def _():
        ch, cl = split(cinv_ref[0][:, :RANK] * 0.125)
        rh, rl = split(rt_ref[0])
        right = nn(jnp.concatenate([ch, cl], axis=1), jnp.concatenate([rh, rh], axis=0)) + nn(ch, rl)
        h, l = split(right)
        r3[0:RANK] = h
        r3[RANK : 2 * RANK] = h
        r3[2 * RANK :] = l
        next_ref[0] = right.T
        oh, ol = split(ot_ref[0].T)
        o3[...] = jnp.concatenate([oh, ol, oh], axis=1)

    approx = nn(o3[pl.ds(i * RB, RB), :], r3[...])
    upd_ref[0] = approx.astype(BF16)
    new_ref[0] = grad_ref[0].astype(F32) + err_ref[0] - approx


def on_device(grad_kv, error_kv, basis_kv):
    grad, err = grad_kv[0], error_kv[0]
    dma = pltpu.SemaphoreType.DMA
    anyspec = pl.BlockSpec(memory_space=pl.ANY)
    vspec = pl.BlockSpec(memory_space=pltpu.VMEM)
    rt, cinv, ot = pl.pallas_call(
        comm_kernel,
        name="exchange",
        out_shape=(
            jax.ShapeDtypeStruct((2, RANK, KVC), F32),
            jax.ShapeDtypeStruct((2, RANK, 128), F32),
            jax.ShapeDtypeStruct((2, RANK, ROWS), F32),
        ),
        in_specs=[anyspec] * 3,
        out_specs=(vspec,) * 3,
        scratch_shapes=[
            pltpu.VMEM((ROWS, KVC), BF16),
            pltpu.VMEM((ROWS, KVC), F32),
            pltpu.VMEM((ROWS, KVC), BF16),
            pltpu.VMEM((ROWS, KVC), F32),
            pltpu.VMEM((KVC, RANK), F32),
            pltpu.VMEM((NQ, QR, KVC), F32),
            pltpu.VMEM((NQ, QR, KVC), F32),
            pltpu.VMEM((ROWS, KVC), BF16),
            pltpu.VMEM((ROWS, KVC), BF16),
            pltpu.VMEM((RANK, ROWS), F32),
            pltpu.VMEM((RANK, ROWS), F32),
            pltpu.VMEM((RANK, ROWS), F32),
            pltpu.VMEM((RANK, ROWS), F32),
            pltpu.VMEM((RANK // 2, 128), F32),
            pltpu.VMEM((NZ - 1, RANK // 2, 128), F32),
            pltpu.VMEM((RANK // 2, 128), F32),
            pltpu.VMEM((NX - 1, RANK // 2, 128), F32),
            pltpu.VMEM((RANK, KVC), F32),
            pltpu.VMEM((NCH, len(PLANE), 8, PW), F32),
            pltpu.VMEM((NCH, 8, PW), F32),
            pltpu.VMEM((NCH, NZ - 1, 8, PW), F32),
            pltpu.VMEM((NCH, 8, PW), F32),
            pltpu.VMEM((RANK, 128), F32),
            dma((2 * NQ + 3,)),
            dma((NQ,)),
            dma((NQ,)),
            dma((4,)),
            dma((4,)),
            dma((2,)),
            dma((2,)),
        ]
        + [dma((NCH,))] * 8
        + [dma((2,)), dma((2,))],
        compiler_params=pltpu.CompilerParams(
            collective_id=0, has_side_effects=True, vmem_limit_bytes=40 << 20
        ),
    )(grad, err, basis_kv)
    whole = lambda shape: pl.BlockSpec((1, *shape), lambda m, i: (m, 0, 0))
    tile = pl.BlockSpec((1, RB, KVC), lambda m, i: (m, i, 0))
    upd, new, nxt = pl.pallas_call(
        out_kernel,
        name="decompress",
        grid=(2, ROWS // RB),
        out_shape=(
            jax.ShapeDtypeStruct((2, ROWS, KVC), BF16),
            jax.ShapeDtypeStruct((2, ROWS, KVC), F32),
            jax.ShapeDtypeStruct((2, KVC, RANK), F32),
        ),
        in_specs=[tile, tile, whole((RANK, KVC)), whole((RANK, 128)), whole((RANK, ROWS))],
        out_specs=(tile, tile, whole((KVC, RANK))),
        scratch_shapes=[pltpu.VMEM((3 * RANK, KVC), BF16), pltpu.VMEM((ROWS, 3 * RANK), BF16)],
    )(grad, err, rt, cinv, ot)
    return upd, new[None], nxt


def solution(mesh):
    placed = (P("rep", None, "shard", None), P("rep", None, "shard", None), P())
    return jax.shard_map(
        on_device,
        mesh=mesh,
        in_specs=placed,
        out_specs=(P(None, "shard", None), P("rep", None, "shard", None), P()),
        check_vma=False,
    )
```

```python
import functools

import jax
import jax.numpy as jnp
from jax import lax
from jax.experimental import pallas as pl
from jax.experimental.pallas import tpu as pltpu
from jax.sharding import PartitionSpec as P

MESH = pl.DeviceIdType.MESH
F32 = jnp.float32
BF16 = jnp.bfloat16
HIGHEST = lax.Precision.HIGHEST

ROWS = 256
KVC = 1024
RANK = 64
NX, NY, NZ = 4, 4, 8
NQ = 4
QR = ROWS // NQ
NCH = 2
CW = KVC // NCH
PW = CW // 2
PLANE = [(dx, dy) for dx in range(NX) for dy in range(NY) if dx or dy]


def split(x):
    hi = x.astype(BF16)
    return hi, (x - hi.astype(F32)).astype(BF16)


def nt(a, b, **kw):
    return lax.dot_general(a, b, (((1,), (1,)), ((), ())), preferred_element_type=F32, **kw)


def nn(a, b, **kw):
    return lax.dot_general(a, b, (((1,), (0,)), ((), ())), preferred_element_type=F32, **kw)


def factor_panels(blocks, panels):
    sub_i = lax.broadcasted_iota(jnp.int32, (8, 128), 0)
    for kb in panels:
        live = range(kb, 8)
        cols = {
            b: [jnp.broadcast_to(blocks[b][:, 8 * kb + j : 8 * kb + j + 1], (8, 128)) for j in range(8)]
            for b in live
        }
        for s in range(8):
            row = jnp.broadcast_to(blocks[kb][s : s + 1, :], (8, 128))
            inv = 1.0 / jnp.broadcast_to(cols[kb][s][s : s + 1, :], (8, 128))
            heads = [jnp.broadcast_to(cols[kb][j][s : s + 1, :], (8, 128)) for j in range(8)]
            for b in live:
                f = cols[b][s] * inv
                if b == kb:
                    f = jnp.where(sub_i > s, f, 0.0)
                blocks[b] = blocks[b] - f * row
                for j in range(s + 1, 8):
                    cols[b][j] = cols[b][j] - f * heads[j]
    return blocks


def comm_kernel(
    grad_ref, err_ref, basis_ref,
    rt_out, cinv_out, ot_out, mer,
    g_o, e_o, g_s, e_s, b_v, pin, p_hi, p_lo,
    l1, lr1, l2, lr2,
    gz_b, gz_r, gx_b, gx_r,
    rs_b, rs_r, z_b, z_r, ag_b, w_b,
    ld, px_s, px_r, l_s, l_r, g_ss, g_rs, rs_s, rs_rs, z_s, z_rs, ag_s, ag_rs, fw_s, fw_r, co_s, co_r,
    near2, near3, near4,
):
    rep, shard = lax.axis_index("rep"), lax.axis_index("shard")
    y, c = rep // 2, rep % 2
    z, x = shard // NX, shard % NX

    def dev(yy, zz, xx, cc=None):
        return (yy * 2 + (c if cc is None else cc), zz * NX + xx)

    partner = dev(y, z, x, 1 - c)
    plane = [(dx, dy, dev((y + dy) % NY, z, (x + dx) % NX)) for dx, dy in PLANE]
    zline = [dev(y, (z + d) % NZ, x) for d in range(1, NZ)]
    xline = [dev(y, z, (x + d) % NX) for d in range(1, NX)]

    def remote(src, dst, ss, rs, to):
        copy = pltpu.make_async_remote_copy(
            src_ref=src, dst_ref=dst, send_sem=ss, recv_sem=rs, device_id=to, device_id_type=MESH
        )
        copy.start()
        return copy

    def wait_bytes(ref, sem):
        pltpu.make_async_copy(ref, ref, sem).wait()

    oc = 1 - c
    loads = []
    for q in range(NQ):
        rows = pl.ds(q * QR, QR)
        pair = []
        for k, (hbm, buf) in enumerate(((grad_ref, g_o), (err_ref, e_o))):
            cp = pltpu.make_async_copy(hbm.at[oc, rows, :], buf.at[rows, :], ld.at[2 * q + k])
            cp.start()
            pair.append(cp)
        loads.append(pair)
    own_b = pltpu.make_async_copy(basis_ref.at[c], b_v, ld.at[2 * NQ])
    own_b.start()
    own_g = pltpu.make_async_copy(grad_ref.at[c], g_s, ld.at[2 * NQ + 1])
    own_g.start()
    own_e = pltpu.make_async_copy(err_ref.at[c], e_s, ld.at[2 * NQ + 2])
    own_e.start()

    near = [
        dev(y, z, (x + 1) % NX), dev(y, z, (x + NX - 1) % NX),
        dev((y + 1) % NY, z, x), dev((y + NY - 1) % NY, z, x),
        dev(y, (z + 1) % NZ, x), dev(y, (z + NZ - 1) % NZ, x),
    ]

    def tell(sem, peers):
        for d in peers:
            pl.semaphore_signal(sem, inc=1, device_id=d, device_id_type=MESH)

    barrier = pltpu.get_barrier_semaphore()
    tell(barrier, [partner] + near)
    pl.semaphore_wait(barrier, 1 + len(near))
    tell(near2, near)

    px = []
    for q in range(NQ):
        rows = pl.ds(q * QR, QR)
        loads[q][0].wait()
        loads[q][1].wait()
        mer[oc, rows, :] = g_o[rows, :].astype(F32) + e_o[rows, :]
        px.append(remote(mer.at[oc, rows, :], pin.at[rows, :], px_s.at[q], px_r.at[q], partner))
    own_b.wait()
    bt_h, bt_l = split(b_v[...])
    bt2 = jnp.concatenate([bt_h, bt_l], axis=0)
    own_g.wait()
    own_e.wait()
    mer[c] = g_s[...].astype(F32) + e_s[...]
    pl.semaphore_wait(near2, len(near))
    tell(near3, near)
    for q in range(NQ):
        rows = pl.ds(q * QR, QR)
        px[q].wait_recv()
        h, l = split(mer[c, rows, :] + pin[rows, :])
        p_hi[rows, :] = h
        p_lo[rows, :] = l
    t = nt(bt2, p_hi[...])
    lt = (t[:RANK] + t[RANK:] + nt(bt_h, p_lo[...])) * 0.125
    l1[...] = lt
    flip = y + 1 - 2 * (y % 2)
    side = (y + 3 + 2 * (y % 2)) % NY
    d_flip, d_side = dev(flip, z, x), dev(side, z, x)
    half = RANK // 2
    lo_half, hi_half = pl.ds(0, half), pl.ds(half, half)
    a1 = remote(l1.at[lo_half], lr1.at[lo_half], l_s.at[0], l_r.at[0], d_flip)
    b1 = remote(l1.at[hi_half], lr1.at[hi_half], l_s.at[1], l_r.at[1], d_side)
    pl.semaphore_wait(near3, len(near))
    tell(near4, near)
    a1.wait_recv()
    l2[lo_half, :] = lt[:half] + lr1[lo_half, :]
    a2 = remote(l2.at[lo_half], lr2.at[lo_half], l_s.at[2], l_r.at[2], d_side)
    b1.wait_recv()
    l2[hi_half, :] = lt[half:] + lr1[hi_half, :]
    b2 = remote(l2.at[hi_half], lr2.at[hi_half], l_s.at[3], l_r.at[3], d_flip)
    a2.wait_recv()
    b2.wait_recv()
    lt = l2[...] + lr2[...]
    pl.semaphore_wait(near4, len(near))

    gram = nt(lt, lt, precision=HIGHEST)
    gz_b[...] = jnp.concatenate([gram[: RANK // 2], gram[RANK // 2 :]], axis=1)
    gz = [remote(gz_b, gz_r.at[d], g_ss.at[0], g_rs.at[0], to) for d, to in enumerate(zline)]

    lt_h, lt_l = split(lt)
    lt2 = jnp.concatenate([lt_h, lt_l], axis=0)

    def piece(ref, p, j):
        rows = pl.ds(pl.multiple_of((p // 2) * 8, 8), 8)
        cols = pl.ds(pl.multiple_of(j * CW + (p % 2) * PW, PW), PW)
        return rows, cols

    me = y * NX + x
    for j in range(NCH):
        t = nn(lt2, p_hi[:, j * CW : (j + 1) * CW])
        rs_b[:, j * CW : (j + 1) * CW] = t[:RANK] + t[RANK:] + nn(lt_h, p_lo[:, j * CW : (j + 1) * CW])
        for i, (dx, dy, to) in enumerate(plane):
            at = ((y + dy) % NY) * NX + (x + dx) % NX
            rows, cols = piece(rs_b, at, j)
            remote(rs_b.at[rows, cols], rs_r.at[j, i], rs_s.at[j], rs_rs.at[j], to)

    def gram_z():
        wait_bytes(gz_r, g_rs.at[0])
        r = [gz_b[...]] + [gz_r[d] for d in range(NZ - 1)]
        gx_b[...] = ((r[0] + r[4]) + (r[2] + r[6])) + ((r[1] + r[5]) + (r[3] + r[7]))
        for d, to in enumerate(xline):
            remote(gx_b, gx_r.at[d], g_ss.at[1], g_rs.at[1], to)

    def sum_rs(j):
        wait_bytes(rs_r.at[j], rs_rs.at[j])
        rows, cols = piece(rs_b, me, j)
        r = [rs_b[rows, cols]] + [rs_r[j, i] for i in range(len(PLANE))]
        while len(r) > 1:
            r = [r[i] + r[i + 1] for i in range(0, len(r), 2)]
        z_b[j] = r[0]
        for d, to in enumerate(zline):
            remote(z_b.at[j], z_r.at[j, d], z_s.at[j], z_rs.at[j], to)

    def sum_z(j):
        wait_bytes(z_r.at[j], z_rs.at[j])
        r = [z_b[j]] + [z_r[j, d] for d in range(NZ - 1)]
        total = ((r[0] + r[4]) + (r[2] + r[6])) + ((r[1] + r[5]) + (r[3] + r[7]))
        rows, cols = piece(rs_b, me, j)
        ag_b[j] = total
        rt_out[c, rows, cols] = total
        for _, _, to in plane:
            remote(ag_b.at[j], rt_out.at[c, rows, cols], ag_s.at[j], ag_rs.at[j], to)

    sum_rs(0)
    gram_z()
    for j in range(1, NCH):
        sum_rs(j)
    wait_bytes(gx_r, g_rs.at[1])
    g = (gx_b[...] + gx_r[1]) + (gx_r[0] + gx_r[2])
    gram = jnp.concatenate([g[:, :RANK], g[:, RANK:]], axis=0)
    ri = lax.broadcasted_iota(jnp.int32, (RANK, RANK), 0)
    ci = lax.broadcasted_iota(jnp.int32, (RANK, RANK), 1)
    w = jnp.concatenate([gram, jnp.where(ri == ci, 1.0, 0.0)], axis=1)
    blocks = [w[8 * b : 8 * b + 8] for b in range(8)]
    blocks = factor_panels(blocks, range(0, 2))
    for j in range(NCH):
        sum_z(j)
    blocks = factor_panels(blocks, range(2, 8))
    w = jnp.concatenate(blocks, axis=0)
    u, low = w[:, :RANK], w[:, RANK:]
    diag = jnp.sum(jnp.where(ri == ci, u, 0.0), axis=1, keepdims=True)
    cinv = low * lax.rsqrt(diag)
    w_b[...] = jnp.concatenate([cinv, jnp.zeros_like(cinv)], axis=1)
    cinv_out[c] = w_b[...]
    ot_out[c] = nn(cinv, lt, precision=HIGHEST)
    remote(cinv_out.at[c], cinv_out.at[c], co_s.at[0], co_r.at[0], partner)
    remote(ot_out.at[c], ot_out.at[c], co_s.at[1], co_r.at[1], partner)
    for j in range(NCH):
        wait_bytes(rs_r.at[j], ag_rs.at[j])
        cols = pl.ds(j * CW, CW)
        remote(rt_out.at[c, :, cols], rt_out.at[c, :, cols], fw_s.at[j], fw_r.at[j], partner)

    wait_bytes(cinv_out.at[oc], co_r.at[0])
    wait_bytes(ot_out.at[oc], co_r.at[1])
    for j in range(NCH):
        wait_bytes(rt_out.at[oc, :, pl.ds(j * CW, CW)], fw_r.at[j])
    for q in range(NQ):
        px[q].wait_send()
    for cp in (a1, b1, a2, b2):
        cp.wait_send()
    wait_bytes(gz_r, g_ss.at[0])
    wait_bytes(gx_r, g_ss.at[1])
    for j in range(NCH):
        wait_bytes(rs_r.at[j], rs_s.at[j])
        wait_bytes(z_r.at[j], z_s.at[j])
        wait_bytes(rs_r.at[j], ag_s.at[j])
        wait_bytes(rt_out.at[c, :, pl.ds(j * CW, CW)], fw_s.at[j])
    wait_bytes(cinv_out.at[c], co_s.at[0])
    wait_bytes(ot_out.at[c], co_s.at[1])


OB = 64


def out_kernel(mer_ref, rt_ref, cinv_ref, ot_ref, upd_ref, new_ref, next_ref, upd, new, nxt, r3, o3, sems):
    started = []

    def out(src, dst, sem):
        copy = pltpu.make_async_copy(src, dst, sem)
        copy.start()
        started.append(copy)

    for m in range(2):
        ch, cl = split(cinv_ref[m][:, :RANK] * 0.125)
        rh, rl = split(rt_ref[m])
        right = nn(jnp.concatenate([ch, cl], axis=1), jnp.concatenate([rh, rh], axis=0)) + nn(ch, rl)
        nxt[m] = right
        out(nxt.at[m], next_ref.at[m], sems.at[0, m])
        h, l = split(right)
        r3[m, 0:RANK] = h
        r3[m, RANK : 2 * RANK] = h
        r3[m, 2 * RANK :] = l
        oh, ol = split(ot_ref[m].T)
        o3[m] = jnp.concatenate([oh, ol, oh], axis=1)
        for i in range(ROWS // OB):
            rows = pl.ds(i * OB, OB)
            approx = nn(o3[m, rows, :], r3[m])
            upd[m, rows, :] = approx.astype(BF16)
            new[m, rows, :] = mer_ref[m, rows, :] - approx
            n = m * (ROWS // OB) + i
            out(upd.at[m, rows, :], upd_ref.at[m, rows, :], sems.at[1, n])
            out(new.at[m, rows, :], new_ref.at[m, rows, :], sems.at[2, n])
    for copy in started:
        copy.wait()


def on_device(grad_kv, error_kv, basis_kv):
    grad, err = grad_kv[0], error_kv[0]
    dma = pltpu.SemaphoreType.DMA
    anyspec = pl.BlockSpec(memory_space=pltpu.HBM)
    vspec = pl.BlockSpec(memory_space=pltpu.VMEM)
    rt, cinv, ot, mer = pl.pallas_call(
        comm_kernel,
        name="exchange",
        out_shape=(
            jax.ShapeDtypeStruct((2, RANK, KVC), F32),
            jax.ShapeDtypeStruct((2, RANK, 128), F32),
            jax.ShapeDtypeStruct((2, RANK, ROWS), F32),
            jax.ShapeDtypeStruct((2, ROWS, KVC), F32),
        ),
        in_specs=[anyspec] * 3,
        out_specs=(vspec,) * 4,
        scratch_shapes=[
            pltpu.VMEM((ROWS, KVC), BF16),
            pltpu.VMEM((ROWS, KVC), F32),
            pltpu.VMEM((ROWS, KVC), BF16),
            pltpu.VMEM((ROWS, KVC), F32),
            pltpu.VMEM((RANK, KVC), F32),
            pltpu.VMEM((ROWS, KVC), F32),
            pltpu.VMEM((ROWS, KVC), BF16),
            pltpu.VMEM((ROWS, KVC), BF16),
            pltpu.VMEM((RANK, ROWS), F32),
            pltpu.VMEM((RANK, ROWS), F32),
            pltpu.VMEM((RANK, ROWS), F32),
            pltpu.VMEM((RANK, ROWS), F32),
            pltpu.VMEM((RANK // 2, 128), F32),
            pltpu.VMEM((NZ - 1, RANK // 2, 128), F32),
            pltpu.VMEM((RANK // 2, 128), F32),
            pltpu.VMEM((NX - 1, RANK // 2, 128), F32),
            pltpu.VMEM((RANK, KVC), F32),
            pltpu.VMEM((NCH, len(PLANE), 8, PW), F32),
            pltpu.VMEM((NCH, 8, PW), F32),
            pltpu.VMEM((NCH, NZ - 1, 8, PW), F32),
            pltpu.VMEM((NCH, 8, PW), F32),
            pltpu.VMEM((RANK, 128), F32),
            dma((2 * NQ + 3,)),
            dma((NQ,)),
            dma((NQ,)),
            dma((4,)),
            dma((4,)),
            dma((2,)),
            dma((2,)),
        ]
        + [dma((NCH,))] * 8
        + [dma((2,)), dma((2,))]
        + [pltpu.SemaphoreType.REGULAR] * 3,
        compiler_params=pltpu.CompilerParams(
            collective_id=0, has_side_effects=True, vmem_limit_bytes=40 << 20
        ),
    )(*(pltpu.with_memory_space_constraint(a, pltpu.HBM) for a in (grad, err, jnp.swapaxes(basis_kv, 1, 2))))
    upd, new, nxt = pl.pallas_call(
        out_kernel,
        name="decompress",
        out_shape=(
            jax.ShapeDtypeStruct((2, ROWS, KVC), BF16),
            jax.ShapeDtypeStruct((2, ROWS, KVC), F32),
            jax.ShapeDtypeStruct((2, RANK, KVC), F32),
        ),
        in_specs=[vspec] * 4,
        out_specs=(anyspec,) * 3,
        scratch_shapes=[
            pltpu.VMEM((2, ROWS, KVC), BF16),
            pltpu.VMEM((2, ROWS, KVC), F32),
            pltpu.VMEM((2, RANK, KVC), F32),
            pltpu.VMEM((2, 3 * RANK, KVC), BF16),
            pltpu.VMEM((2, ROWS, 3 * RANK), BF16),
            dma((3, 2 * ROWS // OB)),
        ],
        compiler_params=pltpu.CompilerParams(vmem_limit_bytes=16 << 20),
    )(mer, rt, cinv, ot)
    return upd, new[None], jnp.swapaxes(nxt, 1, 2)


def solution(mesh):
    placed = (P("rep", None, "shard", None), P("rep", None, "shard", None), P())
    return jax.shard_map(
        on_device,
        mesh=mesh,
        in_specs=placed,
        out_specs=(P(None, "shard", None), P("rep", None, "shard", None), P()),
        check_vma=False,
    )
```

```python
import functools

import jax
import jax.numpy as jnp
from jax import lax
from jax.experimental import pallas as pl
from jax.experimental.pallas import tpu as pltpu
from jax.sharding import PartitionSpec as P

MESH = pl.DeviceIdType.MESH
F32 = jnp.float32
BF16 = jnp.bfloat16
HIGHEST = lax.Precision.HIGHEST

ROWS = 256
KVC = 1024
RANK = 64
NX, NY, NZ = 4, 4, 8
NQ = 4
QR = ROWS // NQ
NCH = 2
CW = KVC // NCH
PW = CW // 2


def hops(d, n):
    return min(d, n - d)


PLANE = sorted(
    ((dx, dy) for dx in range(NX) for dy in range(NY) if dx or dy),
    key=lambda o: -hops(o[0], NX) - hops(o[1], NY),
)
DIST = [hops(dx, NX) + hops(dy, NY) for dx, dy in PLANE]
ZLINE = sorted(range(1, NZ), key=lambda d: -hops(d, NZ))
YLINE = sorted(range(1, NY), key=lambda d: -hops(d, NY))
FAR = max(DIST)


def split(x):
    hi = x.astype(BF16)
    return hi, (x - hi.astype(F32)).astype(BF16)


def nt(a, b, **kw):
    return lax.dot_general(a, b, (((1,), (1,)), ((), ())), preferred_element_type=F32, **kw)


def nn(a, b, **kw):
    return lax.dot_general(a, b, (((1,), (0,)), ((), ())), preferred_element_type=F32, **kw)


def factor_panels(blocks, panels):
    sub_i = lax.broadcasted_iota(jnp.int32, (8, 128), 0)
    for kb in panels:
        live = range(kb, 8)
        cols = {
            b: [jnp.broadcast_to(blocks[b][:, 8 * kb + j : 8 * kb + j + 1], (8, 128)) for j in range(8)]
            for b in live
        }
        for s in range(8):
            row = jnp.broadcast_to(blocks[kb][s : s + 1, :], (8, 128))
            inv = 1.0 / jnp.broadcast_to(cols[kb][s][s : s + 1, :], (8, 128))
            heads = [jnp.broadcast_to(cols[kb][j][s : s + 1, :], (8, 128)) for j in range(8)]
            for b in live:
                f = cols[b][s] * inv
                if b == kb:
                    f = jnp.where(sub_i > s, f, 0.0)
                blocks[b] = blocks[b] - f * row
                for j in range(s + 1, 8):
                    cols[b][j] = cols[b][j] - f * heads[j]
    return blocks


def comm_kernel(
    grad_ref, err_ref, basis_ref,
    rt_out, cinv_out, ot_out, mer,
    g_o, e_o, g_s, e_s, b_v, pin, p_hi, p_lo,
    l1, lr,
    gz_b, gz_r, gx_b, gx_r,
    rs_b, rs_r, z_b, z_r, ag_b, w_b,
    ld, px_s, px_r, l_s, l_r, g_ss, g_rs, rs_s, rs_rs, z_s, z_rs, ag_s, ag_rs, fw_s, fw_r, co_s, co_r,
    near2, near3, near4,
):
    rep, shard = lax.axis_index("rep"), lax.axis_index("shard")
    y, c = rep // 2, rep % 2
    z, x = shard // NX, shard % NX

    def dev(yy, zz, xx, cc=None):
        return (yy * 2 + (c if cc is None else cc), zz * NX + xx)

    partner = dev(y, z, x, 1 - c)
    plane = [(dx, dy, dev((y + dy) % NY, z, (x + dx) % NX)) for dx, dy in PLANE]
    zline = [(d - 1, dev(y, (z + d) % NZ, x)) for d in ZLINE]
    yline = [(d - 1, dev((y + d) % NY, z, x)) for d in YLINE]
    xline = [dev(y, z, (x + d) % NX) for d in range(1, NX)]

    def remote(src, dst, ss, rs, to):
        copy = pltpu.make_async_remote_copy(
            src_ref=src, dst_ref=dst, send_sem=ss, recv_sem=rs, device_id=to, device_id_type=MESH
        )
        copy.start()
        return copy

    def wait_bytes(ref, sem):
        pltpu.make_async_copy(ref, ref, sem).wait()

    oc = 1 - c
    loads = []
    for q in range(NQ):
        rows = pl.ds(q * QR, QR)
        pair = []
        for k, (hbm, buf) in enumerate(((grad_ref, g_o), (err_ref, e_o))):
            cp = pltpu.make_async_copy(hbm.at[oc, rows, :], buf.at[rows, :], ld.at[2 * q + k])
            cp.start()
            pair.append(cp)
        loads.append(pair)
    own_b = pltpu.make_async_copy(basis_ref.at[c], b_v, ld.at[2 * NQ])
    own_b.start()
    own_g = pltpu.make_async_copy(grad_ref.at[c], g_s, ld.at[2 * NQ + 1])
    own_g.start()
    own_e = pltpu.make_async_copy(err_ref.at[c], e_s, ld.at[2 * NQ + 2])
    own_e.start()

    near = [
        dev(y, z, (x + 1) % NX), dev(y, z, (x + NX - 1) % NX),
        dev((y + 1) % NY, z, x), dev((y + NY - 1) % NY, z, x),
        dev(y, (z + 1) % NZ, x), dev(y, (z + NZ - 1) % NZ, x),
    ]

    def tell(sem, peers):
        for d in peers:
            pl.semaphore_signal(sem, inc=1, device_id=d, device_id_type=MESH)

    barrier = pltpu.get_barrier_semaphore()
    tell(barrier, [partner] + near)
    pl.semaphore_wait(barrier, 1 + len(near))
    tell(near2, near)

    px = []
    for q in range(NQ):
        rows = pl.ds(q * QR, QR)
        loads[q][0].wait()
        loads[q][1].wait()
        mer[oc, rows, :] = g_o[rows, :].astype(F32) + e_o[rows, :]
        px.append(remote(mer.at[oc, rows, :], pin.at[rows, :], px_s.at[q], px_r.at[q], partner))
    own_b.wait()
    bt_h, bt_l = split(b_v[...])
    bt2 = jnp.concatenate([bt_h, bt_l], axis=0)
    own_g.wait()
    own_e.wait()
    mer[c] = g_s[...].astype(F32) + e_s[...]
    pl.semaphore_wait(near2, len(near))
    tell(near3, near)
    for q in range(NQ):
        rows = pl.ds(q * QR, QR)
        px[q].wait_recv()
        h, l = split(mer[c, rows, :] + pin[rows, :])
        p_hi[rows, :] = h
        p_lo[rows, :] = l
    t = nt(bt2, p_hi[...])
    lt = (t[:RANK] + t[RANK:] + nt(bt_h, p_lo[...])) * 0.125
    l1[...] = lt
    for d, to in yline:
        remote(l1, lr.at[d], l_s.at[0], l_r.at[0], to)
    pl.semaphore_wait(near3, len(near))
    tell(near4, near)
    wait_bytes(lr, l_r.at[0])
    lt = (lt + lr[1]) + (lr[0] + lr[2])
    pl.semaphore_wait(near4, len(near))

    lt_h, lt_l = split(lt)
    lt2 = jnp.concatenate([lt_h, lt_l], axis=0)

    def piece(ref, p, j):
        rows = pl.ds(pl.multiple_of((p // 2) * 8, 8), 8)
        cols = pl.ds(pl.multiple_of(j * CW + (p % 2) * PW, PW), PW)
        return rows, cols

    me = y * NX + x
    for j in range(NCH):
        t = nn(lt2, p_hi[:, j * CW : (j + 1) * CW])
        rs_b[:, j * CW : (j + 1) * CW] = t[:RANK] + t[RANK:] + nn(lt_h, p_lo[:, j * CW : (j + 1) * CW])
        for i, (dx, dy, to) in enumerate(plane):
            at = ((y + dy) % NY) * NX + (x + dx) % NX
            rows, cols = piece(rs_b, at, j)
            remote(rs_b.at[rows, cols], rs_r.at[j, i], rs_s.at[j], rs_rs.at[j], to)

    gram = nt(lt, lt, precision=HIGHEST)
    gz_b[...] = jnp.concatenate([gram[: RANK // 2], gram[RANK // 2 :]], axis=1)
    for d, to in zline:
        remote(gz_b, gz_r.at[d], g_ss.at[0], g_rs.at[0], to)

    def gram_z():
        wait_bytes(gz_r, g_rs.at[0])
        r = [gz_b[...]] + [gz_r[d] for d in range(NZ - 1)]
        gx_b[...] = ((r[0] + r[4]) + (r[2] + r[6])) + ((r[1] + r[5]) + (r[3] + r[7]))
        for d, to in enumerate(xline):
            remote(gx_b, gx_r.at[d], g_ss.at[1], g_rs.at[1], to)

    def sum_rs(j):
        wait_bytes(rs_r.at[j], rs_rs.at[j])
        rows, cols = piece(rs_b, me, j)
        r = [rs_b[rows, cols]] + [rs_r[j, i] for i in range(len(PLANE))]
        while len(r) > 1:
            r = [r[i] + r[i + 1] for i in range(0, len(r), 2)]
        z_b[j] = r[0]
        for d, to in zline:
            remote(z_b.at[j], z_r.at[j, d], z_s.at[j], z_rs.at[j], to)

    def sum_z(j):
        wait_bytes(z_r.at[j], z_rs.at[j])
        r = [z_b[j]] + [z_r[j, d] for d in range(NZ - 1)]
        total = ((r[0] + r[4]) + (r[2] + r[6])) + ((r[1] + r[5]) + (r[3] + r[7]))
        ag_b[j] = total
        rt_out[c, j, me] = total
        for i, (_, _, to) in enumerate(plane):
            remote(ag_b.at[j], rt_out.at[c, j, me], ag_s.at[j], ag_rs.at[j, DIST[i] - 1], to)
        remote(ag_b.at[j], rt_out.at[c, j, me], fw_s.at[0], fw_r.at[0], partner)

    for j in range(NCH):
        sum_rs(j)
    gram_z()
    for j in range(NCH):
        sum_z(j)
    wait_bytes(gx_r, g_rs.at[1])
    g = (gx_b[...] + gx_r[1]) + (gx_r[0] + gx_r[2])
    gram = jnp.concatenate([g[:, :RANK], g[:, RANK:]], axis=0)
    ri = lax.broadcasted_iota(jnp.int32, (RANK, RANK), 0)
    ci = lax.broadcasted_iota(jnp.int32, (RANK, RANK), 1)
    w = jnp.concatenate([gram, jnp.where(ri == ci, 1.0, 0.0)], axis=1)
    blocks = [w[8 * b : 8 * b + 8] for b in range(8)]
    blocks = factor_panels(blocks, range(8))
    w = jnp.concatenate(blocks, axis=0)
    u, low = w[:, :RANK], w[:, RANK:]
    diag = jnp.sum(jnp.where(ri == ci, u, 0.0), axis=1, keepdims=True)
    cinv = low * lax.rsqrt(diag)
    w_b[...] = jnp.concatenate([cinv, jnp.zeros_like(cinv)], axis=1)
    cinv_out[c] = w_b[...]
    ot_out[c] = nn(cinv, lt, precision=HIGHEST)
    remote(cinv_out.at[c], cinv_out.at[c], co_s.at[0], co_r.at[0], partner)
    remote(ot_out.at[c], ot_out.at[c], co_s.at[1], co_r.at[1], partner)
    for j, k in sorted(((j, k) for j in range(NCH) for k in range(FAR)), key=lambda t: t[1] + 0.7 * t[0]):
        wait_bytes(rs_r.at[j, pl.ds(0, DIST.count(k + 1))], ag_rs.at[j, k])
        for (dx, dy, _), n in zip(plane, DIST):
            if n == k + 1:
                at = ((y + dy) % NY) * NX + (x + dx) % NX
                remote(rt_out.at[c, j, at], rt_out.at[c, j, at], fw_s.at[0], fw_r.at[0], partner)

    wait_bytes(cinv_out.at[oc], co_r.at[0])
    wait_bytes(ot_out.at[oc], co_r.at[1])
    wait_bytes(rt_out.at[oc], fw_r.at[0])
    for q in range(NQ):
        px[q].wait_send()
    wait_bytes(lr, l_s.at[0])
    wait_bytes(gz_r, g_ss.at[0])
    wait_bytes(gx_r, g_ss.at[1])
    for j in range(NCH):
        wait_bytes(rs_r.at[j], rs_s.at[j])
        wait_bytes(z_r.at[j], z_s.at[j])
        wait_bytes(rs_r.at[j], ag_s.at[j])
    wait_bytes(rt_out.at[c], fw_s.at[0])
    wait_bytes(cinv_out.at[c], co_s.at[0])
    wait_bytes(ot_out.at[c], co_s.at[1])


OB = 64


def out_kernel(mer_ref, rt_ref, cinv_ref, ot_ref, upd_ref, new_ref, next_ref, upd, new, nxt, r3, o3, sems):
    started = []

    def out(src, dst, sem):
        copy = pltpu.make_async_copy(src, dst, sem)
        copy.start()
        started.append(copy)

    for m in range(2):
        ch, cl = split(cinv_ref[m][:, :RANK] * 0.125)
        raw = jnp.concatenate(
            [
                jnp.concatenate([rt_ref[m, j, 2 * k + h] for j in range(NCH) for h in range(2)], axis=1)
                for k in range(RANK // 8)
            ],
            axis=0,
        )
        rh, rl = split(raw)
        right = nn(jnp.concatenate([ch, cl], axis=1), jnp.concatenate([rh, rh], axis=0)) + nn(ch, rl)
        nxt[m] = right
        out(nxt.at[m], next_ref.at[m], sems.at[0, m])
        h, l = split(right)
        r3[m, 0:RANK] = h
        r3[m, RANK : 2 * RANK] = h
        r3[m, 2 * RANK :] = l
        oh, ol = split(ot_ref[m].T)
        o3[m] = jnp.concatenate([oh, ol, oh], axis=1)
        for i in range(ROWS // OB):
            rows = pl.ds(i * OB, OB)
            approx = nn(o3[m, rows, :], r3[m])
            upd[m, rows, :] = approx.astype(BF16)
            new[m, rows, :] = mer_ref[m, rows, :] - approx
            n = m * (ROWS // OB) + i
            out(upd.at[m, rows, :], upd_ref.at[m, rows, :], sems.at[1, n])
            out(new.at[m, rows, :], new_ref.at[m, rows, :], sems.at[2, n])
    for copy in started:
        copy.wait()


def on_device(grad_kv, error_kv, basis_kv):
    grad, err = grad_kv[0], error_kv[0]
    dma = pltpu.SemaphoreType.DMA
    anyspec = pl.BlockSpec(memory_space=pltpu.HBM)
    vspec = pl.BlockSpec(memory_space=pltpu.VMEM)
    rt, cinv, ot, mer = pl.pallas_call(
        comm_kernel,
        name="exchange",
        out_shape=(
            jax.ShapeDtypeStruct((2, NCH, NX * NY, 8, PW), F32),
            jax.ShapeDtypeStruct((2, RANK, 128), F32),
            jax.ShapeDtypeStruct((2, RANK, ROWS), F32),
            jax.ShapeDtypeStruct((2, ROWS, KVC), F32),
        ),
        in_specs=[anyspec] * 3,
        out_specs=(vspec,) * 4,
        scratch_shapes=[
            pltpu.VMEM((ROWS, KVC), BF16),
            pltpu.VMEM((ROWS, KVC), F32),
            pltpu.VMEM((ROWS, KVC), BF16),
            pltpu.VMEM((ROWS, KVC), F32),
            pltpu.VMEM((RANK, KVC), F32),
            pltpu.VMEM((ROWS, KVC), F32),
            pltpu.VMEM((ROWS, KVC), BF16),
            pltpu.VMEM((ROWS, KVC), BF16),
            pltpu.VMEM((RANK, ROWS), F32),
            pltpu.VMEM((NY - 1, RANK, ROWS), F32),
            pltpu.VMEM((RANK // 2, 128), F32),
            pltpu.VMEM((NZ - 1, RANK // 2, 128), F32),
            pltpu.VMEM((RANK // 2, 128), F32),
            pltpu.VMEM((NX - 1, RANK // 2, 128), F32),
            pltpu.VMEM((RANK, KVC), F32),
            pltpu.VMEM((NCH, len(PLANE), 8, PW), F32),
            pltpu.VMEM((NCH, 8, PW), F32),
            pltpu.VMEM((NCH, NZ - 1, 8, PW), F32),
            pltpu.VMEM((NCH, 8, PW), F32),
            pltpu.VMEM((RANK, 128), F32),
            dma((2 * NQ + 3,)),
            dma((NQ,)),
            dma((NQ,)),
            dma((1,)),
            dma((1,)),
            dma((2,)),
            dma((2,)),
        ]
        + [dma((NCH,))] * 5
        + [dma((NCH, FAR)), dma((1,)), dma((1,))]
        + [dma((2,)), dma((2,))]
        + [pltpu.SemaphoreType.REGULAR] * 3,
        compiler_params=pltpu.CompilerParams(
            collective_id=0, has_side_effects=True, vmem_limit_bytes=40 << 20
        ),
    )(*(pltpu.with_memory_space_constraint(a, pltpu.HBM) for a in (grad, err, jnp.swapaxes(basis_kv, 1, 2))))
    upd, new, nxt = pl.pallas_call(
        out_kernel,
        name="decompress",
        out_shape=(
            jax.ShapeDtypeStruct((2, ROWS, KVC), BF16),
            jax.ShapeDtypeStruct((2, ROWS, KVC), F32),
            jax.ShapeDtypeStruct((2, RANK, KVC), F32),
        ),
        in_specs=[vspec] * 4,
        out_specs=(anyspec,) * 3,
        scratch_shapes=[
            pltpu.VMEM((2, ROWS, KVC), BF16),
            pltpu.VMEM((2, ROWS, KVC), F32),
            pltpu.VMEM((2, RANK, KVC), F32),
            pltpu.VMEM((2, 3 * RANK, KVC), BF16),
            pltpu.VMEM((2, ROWS, 3 * RANK), BF16),
            dma((3, 2 * ROWS // OB)),
        ],
        compiler_params=pltpu.CompilerParams(vmem_limit_bytes=16 << 20),
    )(mer, rt, cinv, ot)
    return upd, new[None], jnp.swapaxes(nxt, 1, 2)


def solution(mesh):
    placed = (P("rep", None, "shard", None), P("rep", None, "shard", None), P())
    return jax.shard_map(
        on_device,
        mesh=mesh,
        in_specs=placed,
        out_specs=(P(None, "shard", None), P("rep", None, "shard", None), P()),
        check_vma=False,
    )
```

```python
import functools

import jax
import jax.numpy as jnp
from jax import lax
from jax.experimental import pallas as pl
from jax.experimental.pallas import tpu as pltpu
from jax.sharding import PartitionSpec as P

MESH = pl.DeviceIdType.MESH
F32 = jnp.float32
BF16 = jnp.bfloat16
HIGHEST = lax.Precision.HIGHEST

ROWS = 256
KVC = 1024
RANK = 64
NX, NY, NZ = 4, 4, 8
NQ = 2
QR = ROWS // NQ
NCH = 4
KR = RANK // NCH
CPR = NX * NY * 8 // KR
PW = KVC // CPR


def hops(d, n):
    return min(d, n - d)


PLANE = sorted(
    ((dx, dy) for dx in range(NX) for dy in range(NY) if dx or dy),
    key=lambda o: -hops(o[0], NX) - hops(o[1], NY),
)
DIST = [hops(dx, NX) + hops(dy, NY) for dx, dy in PLANE]
ZLINE = sorted(range(1, NZ), key=lambda d: -hops(d, NZ))
YLINE = sorted(range(1, NY), key=lambda d: -hops(d, NY))
FAR = max(DIST)
NP = len(PLANE)


def split(x):
    hi = x.astype(BF16)
    return hi, (x - hi.astype(F32)).astype(BF16)


def nt(a, b, **kw):
    return lax.dot_general(a, b, (((1,), (1,)), ((), ())), preferred_element_type=F32, **kw)


def nn(a, b, **kw):
    return lax.dot_general(a, b, (((1,), (0,)), ((), ())), preferred_element_type=F32, **kw)


def factor_panels(blocks, panels):
    sub_i = lax.broadcasted_iota(jnp.int32, (8, 128), 0)
    for kb in panels:
        live = range(kb, 8)
        cols = {
            b: [jnp.broadcast_to(blocks[b][:, 8 * kb + j : 8 * kb + j + 1], (8, 128)) for j in range(8)]
            for b in live
        }
        for s in range(8):
            row = jnp.broadcast_to(blocks[kb][s : s + 1, :], (8, 128))
            inv = 1.0 / jnp.broadcast_to(cols[kb][s][s : s + 1, :], (8, 128))
            heads = [jnp.broadcast_to(cols[kb][j][s : s + 1, :], (8, 128)) for j in range(8)]
            for b in live:
                f = cols[b][s] * inv
                if b == kb:
                    f = jnp.where(sub_i > s, f, 0.0)
                blocks[b] = blocks[b] - f * row
                for j in range(s + 1, 8):
                    cols[b][j] = cols[b][j] - f * heads[j]
    return blocks


def comm_kernel(
    grad_ref, err_ref, basis_ref,
    rt_out, cinv_out, ot_out, mer,
    g_o, e_o, g_s, e_s, b_v, pin, p_hi, p_lo,
    l1, lr,
    gz_b, gz_r, gx_b, gx_r,
    rs_b, rs_r, z_b, z_r, ag_b, w_b,
    ld, px_s, px_r, l_s, l_r, g_ss, g_rs, rs_s, rs_rs, z_s, z_rs, ag_s, ag_rs, fw_s, fw_r, co_s, co_r,
    near2, near3, near4, near5,
):
    rep, shard = lax.axis_index("rep"), lax.axis_index("shard")
    y, c = rep // 2, rep % 2
    z, x = shard // NX, shard % NX

    def dev(yy, zz, xx, cc=None):
        return (yy * 2 + (c if cc is None else cc), zz * NX + xx)

    partner = dev(y, z, x, 1 - c)
    plane = [(dx, dy, dev((y + dy) % NY, z, (x + dx) % NX, 1)) for dx, dy in PLANE]
    zline = [(d - 1, dev(y, (z + d) % NZ, x)) for d in ZLINE]
    yline = [(d - 1, dev((y + d) % NY, z, x)) for d in YLINE]
    xline = [dev(y, z, (x + d) % NX) for d in range(1, NX)]

    def remote(src, dst, ss, rs, to):
        copy = pltpu.make_async_remote_copy(
            src_ref=src, dst_ref=dst, send_sem=ss, recv_sem=rs, device_id=to, device_id_type=MESH
        )
        copy.start()
        return copy

    def wait_bytes(ref, sem):
        pltpu.make_async_copy(ref, ref, sem).wait()

    oc = 1 - c
    loads = []
    for q in range(NQ):
        rows = pl.ds(q * QR, QR)
        pair = []
        for k, (hbm, buf) in enumerate(((grad_ref, g_o), (err_ref, e_o))):
            cp = pltpu.make_async_copy(hbm.at[oc, rows, :], buf.at[rows, :], ld.at[2 * q + k])
            cp.start()
            pair.append(cp)
        loads.append(pair)
    own_b = pltpu.make_async_copy(basis_ref.at[c], b_v, ld.at[2 * NQ])
    own_b.start()
    own_g = pltpu.make_async_copy(grad_ref.at[c], g_s, ld.at[2 * NQ + 1])
    own_g.start()
    own_e = pltpu.make_async_copy(err_ref.at[c], e_s, ld.at[2 * NQ + 2])
    own_e.start()

    near = [
        dev(y, z, (x + 1) % NX), dev(y, z, (x + NX - 1) % NX),
        dev((y + 1) % NY, z, x), dev((y + NY - 1) % NY, z, x),
        dev(y, (z + 1) % NZ, x), dev(y, (z + NZ - 1) % NZ, x),
    ]

    def tell(sem, peers):
        for d in peers:
            pl.semaphore_signal(sem, inc=1, device_id=d, device_id_type=MESH)

    barrier = pltpu.get_barrier_semaphore()
    tell(barrier, [partner] + near)
    pl.semaphore_wait(barrier, 1 + len(near))
    tell(near2, near)

    px = []
    for q in range(NQ):
        rows = pl.ds(q * QR, QR)
        loads[q][0].wait()
        loads[q][1].wait()
        mer[oc, rows, :] = g_o[rows, :].astype(F32) + e_o[rows, :]
        px.append(remote(mer.at[oc, rows, :], pin.at[rows, :], px_s.at[q], px_r.at[q], partner))
    own_b.wait()
    bt_h, bt_l = split(b_v[...])
    bt2 = jnp.concatenate([bt_h, bt_l], axis=0)
    own_g.wait()
    own_e.wait()
    mer[c] = g_s[...].astype(F32) + e_s[...]
    pl.semaphore_wait(near2, len(near))
    tell(near3, near)
    for q in range(NQ):
        rows = pl.ds(q * QR, QR)
        px[q].wait_recv()
        h, l = split(mer[c, rows, :] + pin[rows, :])
        p_hi[rows, :] = h
        p_lo[rows, :] = l
    pl.semaphore_wait(near3, len(near))
    tell(near4, near)
    t = nt(bt2, p_hi[...])
    lt = (t[:RANK] + t[RANK:] + nt(bt_h, p_lo[...])) * 0.125
    l1[...] = lt
    for j in range(NCH):
        rows = pl.ds(j * KR, KR)
        for d, to in yline:
            remote(l1.at[rows], lr.at[d, rows], l_s.at[j], l_r.at[j], to)
    pl.semaphore_wait(near4, len(near))
    tell(near5, near)

    def piece(p, j):
        rows = pl.ds(pl.multiple_of(j * KR + (p // CPR) * 8, 8), 8)
        cols = pl.ds(pl.multiple_of((p % CPR) * PW, PW), PW)
        return rows, cols

    me = y * NX + x
    ltj = []
    for j in range(NCH):
        rows = slice(j * KR, (j + 1) * KR)
        wait_bytes(lr.at[:, pl.ds(j * KR, KR)], l_r.at[j])
        part = (lt[rows] + lr[1, rows]) + (lr[0, rows] + lr[2, rows])
        ltj.append(part)
        h, l = split(part)
        t = nn(jnp.concatenate([h, l], axis=0), p_hi[...])
        rs_b[rows, :] = t[:KR] + t[KR:] + nn(h, p_lo[...])
        if j == 0:
            pl.semaphore_wait(near5, len(near))
        for i, (dx, dy, to) in enumerate(plane):
            at = ((y + dy) % NY) * NX + (x + dx) % NX
            rows, cols = piece(at, j)
            remote(rs_b.at[rows, cols], rs_r.at[c, j, i], rs_s.at[j], rs_rs.at[c, j], to)

        @pl.when(c == 0)
        def _():
            rows, cols = piece(me, j)
            remote(rs_b.at[rows, cols], rs_r.at[0, j, NP], rs_s.at[j], rs_rs.at[0, j], partner)

    lt = jnp.concatenate(ltj, axis=0)
    gram = nt(lt, lt, precision=HIGHEST)
    gz_b[...] = jnp.concatenate([gram[: RANK // 2], gram[RANK // 2 :]], axis=1)
    for d, to in zline:
        remote(gz_b, gz_r.at[d], g_ss.at[0], g_rs.at[0], to)

    def gram_z():
        wait_bytes(gz_r, g_rs.at[0])
        r = [gz_b[...]] + [gz_r[d] for d in range(NZ - 1)]
        gx_b[...] = ((r[0] + r[4]) + (r[2] + r[6])) + ((r[1] + r[5]) + (r[3] + r[7]))
        for d, to in enumerate(xline):
            remote(gx_b, gx_r.at[d], g_ss.at[1], g_rs.at[1], to)

    def tree(r):
        while len(r) > 1:
            r = [r[i] + r[i + 1] for i in range(0, len(r), 2)]
        return r[0]

    @pl.when(c == 1)
    def _():
        for m in (1, 0):
            for j in range(NCH):
                if m == 1:
                    wait_bytes(rs_r.at[m, j, pl.ds(0, NP)], rs_rs.at[m, j])
                    rows, cols = piece(me, j)
                    last = rs_b[rows, cols]
                else:
                    wait_bytes(rs_r.at[m, j], rs_rs.at[m, j])
                    last = rs_r[m, j, NP]
                total = tree([rs_r[m, j, i] for i in range(NP)] + [last])
                z_b[m, j] = total
                for d in ZLINE:
                    remote(z_b.at[m, j], z_r.at[j, d], z_s.at[m, j], z_rs.at[j], dev(y, (z + d) % NZ, x, m))
                if m == 1:
                    z_r[j, 0] = total
                else:
                    remote(z_b.at[m, j], z_r.at[j, 0], z_s.at[m, j], z_rs.at[j], partner)

    gram_z()
    for j in range(NCH):

        @pl.when(c == 1)
        def _():
            wait_bytes(z_r.at[j, pl.ds(1, NZ - 1)], z_rs.at[j])

        @pl.when(c == 0)
        def _():
            wait_bytes(z_r.at[j], z_rs.at[j])

        r = [z_r[j, d] for d in range(NZ)]
        total = ((r[0] + r[4]) + (r[2] + r[6])) + ((r[1] + r[5]) + (r[3] + r[7]))
        ag_b[j] = total
        rt_out[c, j, me] = total
        for i, (_, _, to) in enumerate(plane):
            remote(ag_b.at[j], rt_out.at[c, j, me], ag_s.at[j], ag_rs.at[c, j, DIST[i] - 1], to)
        remote(ag_b.at[j], rt_out.at[c, j, me], fw_s.at[0], fw_r.at[0], partner)

    wait_bytes(gx_r, g_rs.at[1])
    g = (gx_b[...] + gx_r[1]) + (gx_r[0] + gx_r[2])
    gram = jnp.concatenate([g[:, :RANK], g[:, RANK:]], axis=0)
    ri = lax.broadcasted_iota(jnp.int32, (RANK, RANK), 0)
    ci = lax.broadcasted_iota(jnp.int32, (RANK, RANK), 1)
    w = jnp.concatenate([gram, jnp.where(ri == ci, 1.0, 0.0)], axis=1)
    blocks = [w[8 * b : 8 * b + 8] for b in range(8)]
    blocks = factor_panels(blocks, range(8))
    w = jnp.concatenate(blocks, axis=0)
    u, low = w[:, :RANK], w[:, RANK:]
    diag = jnp.sum(jnp.where(ri == ci, u, 0.0), axis=1, keepdims=True)
    cinv = low * lax.rsqrt(diag)
    w_b[...] = jnp.concatenate([cinv, jnp.zeros_like(cinv)], axis=1)
    cinv_out[c] = w_b[...]
    ot_out[c] = nn(cinv, lt, precision=HIGHEST)
    remote(cinv_out.at[c], cinv_out.at[c], co_s.at[0], co_r.at[0], partner)
    remote(ot_out.at[c], ot_out.at[c], co_s.at[1], co_r.at[1], partner)
    @pl.when(c == 1)
    def _():
        order = sorted(
            ((m, j, k) for m in range(2) for j in range(NCH) for k in range(FAR)),
            key=lambda t: t[2] * 0.6 + 0.5 * t[1] - t[0],
        )
        for m, j, k in order:
            wait_bytes(rs_r.at[m, j, pl.ds(0, DIST.count(k + 1))], ag_rs.at[m, j, k])
            for (dx, dy), n in zip(PLANE, DIST):
                if n == k + 1:
                    at = ((y + dy) % NY) * NX + (x + dx) % NX
                    remote(rt_out.at[m, j, at], rt_out.at[m, j, at], fw_s.at[1], fw_r.at[1], partner)
        wait_bytes(rt_out.at[:, :, pl.ds(0, NP)], fw_s.at[1])
        for m in range(2):
            for j in range(NCH):
                wait_bytes(z_r.at[j, pl.ds(0, NZ - m)], z_s.at[m, j])
                wait_bytes(rs_r.at[1, j, pl.ds(0, NP)], rs_s.at[j]) if m else None

    @pl.when(c == 0)
    def _():
        wait_bytes(rt_out.at[:, :, pl.ds(0, NP)], fw_r.at[1])
        for j in range(NCH):
            wait_bytes(rs_r.at[0, j], rs_s.at[j])

    own = rt_out.at[0, :, 0]
    wait_bytes(own, fw_r.at[0])
    wait_bytes(own, fw_s.at[0])
    wait_bytes(cinv_out.at[oc], co_r.at[0])
    wait_bytes(ot_out.at[oc], co_r.at[1])
    for q in range(NQ):
        px[q].wait_send()
    for j in range(NCH):
        wait_bytes(lr.at[:, pl.ds(j * KR, KR)], l_s.at[j])
    wait_bytes(gz_r, g_ss.at[0])
    wait_bytes(gx_r, g_ss.at[1])
    for j in range(NCH):
        wait_bytes(rs_r.at[0, j, pl.ds(0, NP)], ag_s.at[j])
    wait_bytes(cinv_out.at[c], co_s.at[0])
    wait_bytes(ot_out.at[c], co_s.at[1])


OB = 64


def out_kernel(mer_ref, rt_ref, cinv_ref, ot_ref, upd_ref, new_ref, next_ref, upd, new, nxt, r3, o3, sems):
    started = []

    def out(src, dst, sem):
        copy = pltpu.make_async_copy(src, dst, sem)
        copy.start()
        started.append(copy)

    for m in range(2):
        ch, cl = split(cinv_ref[m][:, :RANK] * 0.125)
        raw = jnp.concatenate(
            [
                jnp.concatenate([rt_ref[m, j, g * CPR + h] for h in range(CPR)], axis=1)
                for j in range(NCH)
                for g in range(KR // 8)
            ],
            axis=0,
        )
        rh, rl = split(raw)
        right = nn(jnp.concatenate([ch, cl], axis=1), jnp.concatenate([rh, rh], axis=0)) + nn(ch, rl)
        nxt[m] = right
        out(nxt.at[m], next_ref.at[m], sems.at[0, m])
        h, l = split(right)
        r3[m, 0:RANK] = h
        r3[m, RANK : 2 * RANK] = h
        r3[m, 2 * RANK :] = l
        oh, ol = split(ot_ref[m].T)
        o3[m] = jnp.concatenate([oh, ol, oh], axis=1)
        for i in range(ROWS // OB):
            rows = pl.ds(i * OB, OB)
            approx = nn(o3[m, rows, :], r3[m])
            upd[m, rows, :] = approx.astype(BF16)
            new[m, rows, :] = mer_ref[m, rows, :] - approx
            n = m * (ROWS // OB) + i
            out(upd.at[m, rows, :], upd_ref.at[m, rows, :], sems.at[1, n])
            out(new.at[m, rows, :], new_ref.at[m, rows, :], sems.at[2, n])
    for copy in started:
        copy.wait()


def on_device(grad_kv, error_kv, basis_kv):
    grad, err = grad_kv[0], error_kv[0]
    dma = pltpu.SemaphoreType.DMA
    anyspec = pl.BlockSpec(memory_space=pltpu.HBM)
    vspec = pl.BlockSpec(memory_space=pltpu.VMEM)
    rt, cinv, ot, mer = pl.pallas_call(
        comm_kernel,
        name="exchange",
        out_shape=(
            jax.ShapeDtypeStruct((2, NCH, NX * NY, 8, PW), F32),
            jax.ShapeDtypeStruct((2, RANK, 128), F32),
            jax.ShapeDtypeStruct((2, RANK, ROWS), F32),
            jax.ShapeDtypeStruct((2, ROWS, KVC), F32),
        ),
        in_specs=[anyspec] * 3,
        out_specs=(vspec,) * 4,
        scratch_shapes=[
            pltpu.VMEM((ROWS, KVC), BF16),
            pltpu.VMEM((ROWS, KVC), F32),
            pltpu.VMEM((ROWS, KVC), BF16),
            pltpu.VMEM((ROWS, KVC), F32),
            pltpu.VMEM((RANK, KVC), F32),
            pltpu.VMEM((ROWS, KVC), F32),
            pltpu.VMEM((ROWS, KVC), BF16),
            pltpu.VMEM((ROWS, KVC), BF16),
            pltpu.VMEM((RANK, ROWS), F32),
            pltpu.VMEM((NY - 1, RANK, ROWS), F32),
            pltpu.VMEM((RANK // 2, 128), F32),
            pltpu.VMEM((NZ - 1, RANK // 2, 128), F32),
            pltpu.VMEM((RANK // 2, 128), F32),
            pltpu.VMEM((NX - 1, RANK // 2, 128), F32),
            pltpu.VMEM((RANK, KVC), F32),
            pltpu.VMEM((2, NCH, NP + 1, 8, PW), F32),
            pltpu.VMEM((2, NCH, 8, PW), F32),
            pltpu.VMEM((NCH, NZ, 8, PW), F32),
            pltpu.VMEM((NCH, 8, PW), F32),
            pltpu.VMEM((RANK, 128), F32),
            dma((2 * NQ + 3,)),
            dma((NQ,)),
            dma((NQ,)),
            dma((NCH,)),
            dma((NCH,)),
            dma((2,)),
            dma((2,)),
        ]
        + [dma((NCH,)), dma((2, NCH)), dma((2, NCH)), dma((NCH,)), dma((NCH,)), dma((2, NCH, FAR)), dma((2,)), dma((2,))]
        + [dma((2,)), dma((2,))]
        + [pltpu.SemaphoreType.REGULAR] * 4,
        compiler_params=pltpu.CompilerParams(
            collective_id=0, has_side_effects=True, vmem_limit_bytes=40 << 20
        ),
    )(*(pltpu.with_memory_space_constraint(a, pltpu.HBM) for a in (grad, err, jnp.swapaxes(basis_kv, 1, 2))))
    upd, new, nxt = pl.pallas_call(
        out_kernel,
        name="decompress",
        out_shape=(
            jax.ShapeDtypeStruct((2, ROWS, KVC), BF16),
            jax.ShapeDtypeStruct((2, ROWS, KVC), F32),
            jax.ShapeDtypeStruct((2, RANK, KVC), F32),
        ),
        in_specs=[vspec] * 4,
        out_specs=(anyspec,) * 3,
        scratch_shapes=[
            pltpu.VMEM((2, ROWS, KVC), BF16),
            pltpu.VMEM((2, ROWS, KVC), F32),
            pltpu.VMEM((2, RANK, KVC), F32),
            pltpu.VMEM((2, 3 * RANK, KVC), BF16),
            pltpu.VMEM((2, ROWS, 3 * RANK), BF16),
            dma((3, 2 * ROWS // OB)),
        ],
        compiler_params=pltpu.CompilerParams(vmem_limit_bytes=16 << 20),
    )(mer, rt, cinv, ot)
    return upd, new[None], jnp.swapaxes(nxt, 1, 2)


def solution(mesh):
    placed = (P("rep", None, "shard", None), P("rep", None, "shard", None), P())
    return jax.shard_map(
        on_device,
        mesh=mesh,
        in_specs=placed,
        out_specs=(P(None, "shard", None), P("rep", None, "shard", None), P()),
        check_vma=False,
    )
```

```python
import functools

import jax
import jax.numpy as jnp
from jax import lax
from jax.experimental import pallas as pl
from jax.experimental.pallas import tpu as pltpu
from jax.sharding import PartitionSpec as P

MESH = pl.DeviceIdType.MESH
F32 = jnp.float32
BF16 = jnp.bfloat16
HIGHEST = lax.Precision.HIGHEST

ROWS = 256
KVC = 1024
RANK = 64
NX, NY, NZ = 4, 4, 8
NQ = 2
QR = ROWS // NQ
NCH = 2
KR = RANK // NCH
CPR = NX * NY * 8 // KR
PW = KVC // CPR


def hops(d, n):
    return min(d, n - d)


PLANE = sorted(
    ((dx, dy) for dx in range(NX) for dy in range(NY) if dx or dy),
    key=lambda o: -hops(o[0], NX) - hops(o[1], NY),
)
DIST = [hops(dx, NX) + hops(dy, NY) for dx, dy in PLANE]
ZLINE = sorted(range(1, NZ), key=lambda d: -hops(d, NZ))
YLINE = sorted(range(1, NY), key=lambda d: -hops(d, NY))
FAR = max(DIST)
NP = len(PLANE)
NF = NP - DIST.count(FAR)


def split(x):
    hi = x.astype(BF16)
    return hi, (x - hi.astype(F32)).astype(BF16)


def nt(a, b, **kw):
    return lax.dot_general(a, b, (((1,), (1,)), ((), ())), preferred_element_type=F32, **kw)


def nn(a, b, **kw):
    return lax.dot_general(a, b, (((1,), (0,)), ((), ())), preferred_element_type=F32, **kw)


def factor_panels(blocks, panels):
    sub_i = lax.broadcasted_iota(jnp.int32, (8, 128), 0)
    for kb in panels:
        live = range(kb, 8)
        cols = {
            b: [jnp.broadcast_to(blocks[b][:, 8 * kb + j : 8 * kb + j + 1], (8, 128)) for j in range(8)]
            for b in live
        }
        for s in range(8):
            row = jnp.broadcast_to(blocks[kb][s : s + 1, :], (8, 128))
            inv = 1.0 / jnp.broadcast_to(cols[kb][s][s : s + 1, :], (8, 128))
            heads = [jnp.broadcast_to(cols[kb][j][s : s + 1, :], (8, 128)) for j in range(8)]
            for b in live:
                f = cols[b][s] * inv
                if b == kb:
                    f = jnp.where(sub_i > s, f, 0.0)
                blocks[b] = blocks[b] - f * row
                for j in range(s + 1, 8):
                    cols[b][j] = cols[b][j] - f * heads[j]
    return blocks


def comm_kernel(
    grad_ref, err_ref, basis_ref,
    rt_out, cinv_out, ot_out, mer,
    g_o, e_o, g_s, e_s, b_v, pin, p_hi, p_lo,
    l1, lr,
    gz_b, gz_r, gx_b, gx_r,
    rs_b, rs_r, z_b, z_r, ag_b, w_b,
    ld, px_s, px_r, l_s, l_r, g_ss, g_rs, rs_s, rs_rs, z_s, z_rs, ag_s, ag_rs, fw_s, fw_r, dr_s, dr_r, co_s, co_r,
    near2, near3, near4, near5,
):
    rep, shard = lax.axis_index("rep"), lax.axis_index("shard")
    y, c = rep // 2, rep % 2
    z, x = shard // NX, shard % NX

    def dev(yy, zz, xx, cc=None):
        return (yy * 2 + (c if cc is None else cc), zz * NX + xx)

    partner = dev(y, z, x, 1 - c)
    plane = [(dx, dy, dev((y + dy) % NY, z, (x + dx) % NX, 1)) for dx, dy in PLANE]
    zline = [(d - 1, dev(y, (z + d) % NZ, x)) for d in ZLINE]
    yline = [(d - 1, dev((y + d) % NY, z, x)) for d in YLINE]
    xline = [dev(y, z, (x + d) % NX) for d in range(1, NX)]

    def remote(src, dst, ss, rs, to):
        copy = pltpu.make_async_remote_copy(
            src_ref=src, dst_ref=dst, send_sem=ss, recv_sem=rs, device_id=to, device_id_type=MESH
        )
        copy.start()
        return copy

    def wait_bytes(ref, sem):
        pltpu.make_async_copy(ref, ref, sem).wait()

    oc = 1 - c
    loads = []
    for q in range(NQ):
        rows = pl.ds(q * QR, QR)
        pair = []
        for k, (hbm, buf) in enumerate(((grad_ref, g_o), (err_ref, e_o))):
            cp = pltpu.make_async_copy(hbm.at[oc, rows, :], buf.at[rows, :], ld.at[2 * q + k])
            cp.start()
            pair.append(cp)
        loads.append(pair)
    own_b = pltpu.make_async_copy(basis_ref.at[c], b_v, ld.at[2 * NQ])
    own_b.start()
    own_g = pltpu.make_async_copy(grad_ref.at[c], g_s, ld.at[2 * NQ + 1])
    own_g.start()
    own_e = pltpu.make_async_copy(err_ref.at[c], e_s, ld.at[2 * NQ + 2])
    own_e.start()

    near = [
        dev(y, z, (x + 1) % NX), dev(y, z, (x + NX - 1) % NX),
        dev((y + 1) % NY, z, x), dev((y + NY - 1) % NY, z, x),
        dev(y, (z + 1) % NZ, x), dev(y, (z + NZ - 1) % NZ, x),
    ]

    def tell(sem, peers):
        for d in peers:
            pl.semaphore_signal(sem, inc=1, device_id=d, device_id_type=MESH)

    barrier = pltpu.get_barrier_semaphore()
    tell(barrier, [partner] + near)
    pl.semaphore_wait(barrier, 1 + len(near))
    tell(near2, near)

    px = []
    for q in range(NQ):
        rows = pl.ds(q * QR, QR)
        loads[q][0].wait()
        loads[q][1].wait()
        mer[oc, rows, :] = g_o[rows, :].astype(F32) + e_o[rows, :]
        px.append(remote(mer.at[oc, rows, :], pin.at[rows, :], px_s.at[q], px_r.at[q], partner))
    own_b.wait()
    bt_h, bt_l = split(b_v[...])
    bt2 = jnp.concatenate([bt_h, bt_l], axis=0)
    own_g.wait()
    own_e.wait()
    mer[c] = g_s[...].astype(F32) + e_s[...]
    pl.semaphore_wait(near2, len(near))
    tell(near3, near)
    lq = []
    for q in range(NQ):
        rows = pl.ds(q * QR, QR)
        px[q].wait_recv()
        h, l = split(mer[c, rows, :] + pin[rows, :])
        p_hi[rows, :] = h
        p_lo[rows, :] = l
        t = nt(bt2, h)
        lq.append((t[:RANK] + t[RANK:] + nt(bt_h, l)) * 0.125)
        l1[q] = lq[q]
        for d, to in yline:
            remote(l1.at[q], lr.at[d, q], l_s.at[q], l_r.at[q], to)
        if q == 0:
            pl.semaphore_wait(near3, len(near))
            tell(near4, near)
    pl.semaphore_wait(near4, len(near))
    tell(near5, near)
    for q in range(NQ):
        wait_bytes(lr.at[:, q], l_r.at[q])
        lq[q] = (lq[q] + lr[1, q]) + (lr[0, q] + lr[2, q])
    lt = jnp.concatenate(lq, axis=1)

    def piece(p, j):
        rows = pl.ds(pl.multiple_of(j * KR + (p // CPR) * 8, 8), 8)
        cols = pl.ds(pl.multiple_of((p % CPR) * PW, PW), PW)
        return rows, cols

    me = y * NX + x
    for j in range(NCH):
        rows = slice(j * KR, (j + 1) * KR)
        part = lt[rows]
        h, l = split(part)
        t = nn(jnp.concatenate([h, l], axis=0), p_hi[...])
        rs_b[rows, :] = t[:KR] + t[KR:] + nn(h, p_lo[...])
        if j == 0:
            pl.semaphore_wait(near5, len(near))
        for i, (dx, dy, to) in enumerate(plane):
            at = ((y + dy) % NY) * NX + (x + dx) % NX
            rows, cols = piece(at, j)
            remote(rs_b.at[rows, cols], rs_r.at[c, j, i], rs_s.at[j], rs_rs.at[c, j], to)

        @pl.when(c == 0)
        def _():
            rows, cols = piece(me, j)
            remote(rs_b.at[rows, cols], rs_r.at[0, j, NP], rs_s.at[j], rs_rs.at[0, j], partner)

    gram = nt(lt, lt, precision=HIGHEST)
    gz_b[...] = jnp.concatenate([gram[: RANK // 2], gram[RANK // 2 :]], axis=1)
    for d, to in zline:
        remote(gz_b, gz_r.at[d], g_ss.at[0], g_rs.at[0], to)

    def gram_z():
        wait_bytes(gz_r, g_rs.at[0])
        r = [gz_b[...]] + [gz_r[d] for d in range(NZ - 1)]
        gx_b[...] = ((r[0] + r[4]) + (r[2] + r[6])) + ((r[1] + r[5]) + (r[3] + r[7]))
        for d, to in enumerate(xline):
            remote(gx_b, gx_r.at[d], g_ss.at[1], g_rs.at[1], to)

    def tree(r):
        while len(r) > 1:
            r = [r[i] + r[i + 1] for i in range(0, len(r), 2)]
        return r[0]

    @pl.when(c == 1)
    def _():
        for m in (1, 0):
            for j in range(NCH):
                if m == 1:
                    wait_bytes(rs_r.at[m, j, pl.ds(0, NP)], rs_rs.at[m, j])
                    rows, cols = piece(me, j)
                    last = rs_b[rows, cols]
                else:
                    wait_bytes(rs_r.at[m, j], rs_rs.at[m, j])
                    last = rs_r[m, j, NP]
                total = tree([rs_r[m, j, i] for i in range(NP)] + [last])
                z_b[m, j] = total
                for d in ZLINE:
                    remote(z_b.at[m, j], z_r.at[j, d], z_s.at[m, j], z_rs.at[j], dev(y, (z + d) % NZ, x, 1 - m))
                if m == 0:
                    z_r[j, 0] = total
                else:
                    remote(z_b.at[m, j], z_r.at[j, 0], z_s.at[m, j], z_rs.at[j], partner)

    gram_z()
    for j in range(NCH):

        @pl.when(c == 1)
        def _():
            wait_bytes(z_r.at[j, pl.ds(1, NZ - 1)], z_rs.at[j])

        @pl.when(c == 0)
        def _():
            wait_bytes(z_r.at[j], z_rs.at[j])

        r = [z_r[j, d] for d in range(NZ)]
        total = ((r[0] + r[4]) + (r[2] + r[6])) + ((r[1] + r[5]) + (r[3] + r[7]))
        ag_b[j] = total
        rt_out[oc, j, me] = total
        for i, (dx, dy, to) in enumerate(plane):
            if DIST[i] == FAR:
                both = dev((y + dy) % NY, z, (x + dx) % NX, 0)
                remote(ag_b.at[j], rt_out.at[oc, j, me], dr_s.at[0], dr_r.at[0], both)
            remote(ag_b.at[j], rt_out.at[oc, j, me], ag_s.at[j], ag_rs.at[oc, j, DIST[i] - 1], to)
        remote(ag_b.at[j], rt_out.at[oc, j, me], fw_s.at[0], fw_r.at[0], partner)

    wait_bytes(gx_r, g_rs.at[1])
    g = (gx_b[...] + gx_r[1]) + (gx_r[0] + gx_r[2])
    gram = jnp.concatenate([g[:, :RANK], g[:, RANK:]], axis=0)
    ri = lax.broadcasted_iota(jnp.int32, (RANK, RANK), 0)
    ci = lax.broadcasted_iota(jnp.int32, (RANK, RANK), 1)
    w = jnp.concatenate([gram, jnp.where(ri == ci, 1.0, 0.0)], axis=1)
    blocks = [w[8 * b : 8 * b + 8] for b in range(8)]
    blocks = factor_panels(blocks, range(8))
    w = jnp.concatenate(blocks, axis=0)
    u, low = w[:, :RANK], w[:, RANK:]
    diag = jnp.sum(jnp.where(ri == ci, u, 0.0), axis=1, keepdims=True)
    cinv = low * lax.rsqrt(diag)
    w_b[...] = jnp.concatenate([cinv, jnp.zeros_like(cinv)], axis=1)
    cinv_out[c] = w_b[...]
    ot_out[c] = nn(cinv, lt, precision=HIGHEST)
    remote(cinv_out.at[c], cinv_out.at[c], co_s.at[0], co_r.at[0], partner)
    remote(ot_out.at[c], ot_out.at[c], co_s.at[1], co_r.at[1], partner)
    @pl.when(c == 1)
    def _():
        order = sorted(
            ((m, j, k) for m in range(2) for j in range(NCH) for k in range(FAR)),
            key=lambda t: t[2] * 0.6 + 0.3 * t[1] - 0.4 * t[0],
        )
        for m, j, k in order:
            wait_bytes(rs_r.at[m, j, pl.ds(0, DIST.count(k + 1))], ag_rs.at[m, j, k])
            for (dx, dy), n in zip(PLANE, DIST):
                if n == k + 1 < FAR:
                    at = ((y + dy) % NY) * NX + (x + dx) % NX
                    remote(rt_out.at[m, j, at], rt_out.at[m, j, at], fw_s.at[1], fw_r.at[1], partner)
        wait_bytes(rt_out.at[:, :, pl.ds(0, NF)], fw_s.at[1])
        for m in range(2):
            for j in range(NCH):
                wait_bytes(z_r.at[j, pl.ds(0, NZ - 1 + m)], z_s.at[m, j])
                wait_bytes(rs_r.at[1, j, pl.ds(0, NP)], rs_s.at[j]) if m else None

    @pl.when(c == 0)
    def _():
        wait_bytes(rt_out.at[:, :, pl.ds(0, NF)], fw_r.at[1])
        wait_bytes(rt_out.at[:, :, pl.ds(0, NP - NF)], dr_r.at[0])
        for j in range(NCH):
            wait_bytes(rs_r.at[0, j], rs_s.at[j])

    own = rt_out.at[0, :, 0]
    wait_bytes(own, fw_r.at[0])
    wait_bytes(own, fw_s.at[0])
    wait_bytes(rt_out.at[0, :, pl.ds(0, NP - NF)], dr_s.at[0])
    wait_bytes(cinv_out.at[oc], co_r.at[0])
    wait_bytes(ot_out.at[oc], co_r.at[1])
    for q in range(NQ):
        px[q].wait_send()
    for q in range(NQ):
        wait_bytes(lr.at[:, q], l_s.at[q])
    wait_bytes(gz_r, g_ss.at[0])
    wait_bytes(gx_r, g_ss.at[1])
    for j in range(NCH):
        wait_bytes(rs_r.at[0, j, pl.ds(0, NP)], ag_s.at[j])
    wait_bytes(cinv_out.at[c], co_s.at[0])
    wait_bytes(ot_out.at[c], co_s.at[1])


OB = 64


def out_kernel(mer_ref, rt_ref, cinv_ref, ot_ref, upd_ref, new_ref, next_ref, upd, new, nxt, r3, o3, sems):
    started = []

    def out(src, dst, sem):
        copy = pltpu.make_async_copy(src, dst, sem)
        copy.start()
        started.append(copy)

    for m in range(2):
        ch, cl = split(cinv_ref[m][:, :RANK] * 0.125)
        raw = jnp.concatenate(
            [
                jnp.concatenate([rt_ref[m, j, g * CPR + h] for h in range(CPR)], axis=1)
                for j in range(NCH)
                for g in range(KR // 8)
            ],
            axis=0,
        )
        rh, rl = split(raw)
        right = nn(jnp.concatenate([ch, cl], axis=1), jnp.concatenate([rh, rh], axis=0)) + nn(ch, rl)
        nxt[m] = right
        out(nxt.at[m], next_ref.at[m], sems.at[0, m])
        h, l = split(right)
        r3[m, 0:RANK] = h
        r3[m, RANK : 2 * RANK] = h
        r3[m, 2 * RANK :] = l
        oh, ol = split(ot_ref[m].T)
        o3[m] = jnp.concatenate([oh, ol, oh], axis=1)
    for m in range(2):
        for i in range(ROWS // OB):
            rows = pl.ds(i * OB, OB)
            approx = nn(o3[m, rows, :], r3[m])
            upd[m, rows, :] = approx.astype(BF16)
            new[m, rows, :] = mer_ref[m, rows, :] - approx
            n = m * (ROWS // OB) + i
            out(upd.at[m, rows, :], upd_ref.at[m, rows, :], sems.at[1, n])
            out(new.at[m, rows, :], new_ref.at[m, rows, :], sems.at[2, n])
    for copy in started:
        copy.wait()


def on_device(grad_kv, error_kv, basis_kv):
    grad, err = grad_kv[0], error_kv[0]
    dma = pltpu.SemaphoreType.DMA
    anyspec = pl.BlockSpec(memory_space=pltpu.HBM)
    vspec = pl.BlockSpec(memory_space=pltpu.VMEM)
    rt, cinv, ot, mer = pl.pallas_call(
        comm_kernel,
        name="exchange",
        out_shape=(
            jax.ShapeDtypeStruct((2, NCH, NX * NY, 8, PW), F32),
            jax.ShapeDtypeStruct((2, RANK, 128), F32),
            jax.ShapeDtypeStruct((2, RANK, ROWS), F32),
            jax.ShapeDtypeStruct((2, ROWS, KVC), F32),
        ),
        in_specs=[anyspec] * 3,
        out_specs=(vspec,) * 4,
        scratch_shapes=[
            pltpu.VMEM((ROWS, KVC), BF16),
            pltpu.VMEM((ROWS, KVC), F32),
            pltpu.VMEM((ROWS, KVC), BF16),
            pltpu.VMEM((ROWS, KVC), F32),
            pltpu.VMEM((RANK, KVC), F32),
            pltpu.VMEM((ROWS, KVC), F32),
            pltpu.VMEM((ROWS, KVC), BF16),
            pltpu.VMEM((ROWS, KVC), BF16),
            pltpu.VMEM((NQ, RANK, QR), F32),
            pltpu.VMEM((NY - 1, NQ, RANK, QR), F32),
            pltpu.VMEM((RANK // 2, 128), F32),
            pltpu.VMEM((NZ - 1, RANK // 2, 128), F32),
            pltpu.VMEM((RANK // 2, 128), F32),
            pltpu.VMEM((NX - 1, RANK // 2, 128), F32),
            pltpu.VMEM((RANK, KVC), F32),
            pltpu.VMEM((2, NCH, NP + 1, 8, PW), F32),
            pltpu.VMEM((2, NCH, 8, PW), F32),
            pltpu.VMEM((NCH, NZ, 8, PW), F32),
            pltpu.VMEM((NCH, 8, PW), F32),
            pltpu.VMEM((RANK, 128), F32),
            dma((2 * NQ + 3,)),
            dma((NQ,)),
            dma((NQ,)),
            dma((NQ,)),
            dma((NQ,)),
            dma((2,)),
            dma((2,)),
        ]
        + [dma((NCH,)), dma((2, NCH)), dma((2, NCH)), dma((NCH,)), dma((NCH,)), dma((2, NCH, FAR)), dma((2,)), dma((2,)), dma((1,)), dma((1,))]
        + [dma((2,)), dma((2,))]
        + [pltpu.SemaphoreType.REGULAR] * 4,
        compiler_params=pltpu.CompilerParams(
            collective_id=0, has_side_effects=True, vmem_limit_bytes=40 << 20
        ),
    )(*(pltpu.with_memory_space_constraint(a, pltpu.HBM) for a in (grad, err, jnp.swapaxes(basis_kv, 1, 2))))
    upd, new, nxt = pl.pallas_call(
        out_kernel,
        name="decompress",
        out_shape=(
            jax.ShapeDtypeStruct((2, ROWS, KVC), BF16),
            jax.ShapeDtypeStruct((2, ROWS, KVC), F32),
            jax.ShapeDtypeStruct((2, RANK, KVC), F32),
        ),
        in_specs=[vspec] * 4,
        out_specs=(anyspec,) * 3,
        scratch_shapes=[
            pltpu.VMEM((2, ROWS, KVC), BF16),
            pltpu.VMEM((2, ROWS, KVC), F32),
            pltpu.VMEM((2, RANK, KVC), F32),
            pltpu.VMEM((2, 3 * RANK, KVC), BF16),
            pltpu.VMEM((2, ROWS, 3 * RANK), BF16),
            dma((3, 2 * ROWS // OB)),
        ],
        compiler_params=pltpu.CompilerParams(vmem_limit_bytes=16 << 20),
    )(mer, rt, cinv, ot)
    return upd, new[None], jnp.swapaxes(nxt, 1, 2)


def solution(mesh):
    placed = (P("rep", None, "shard", None), P("rep", None, "shard", None), P())
    return jax.shard_map(
        on_device,
        mesh=mesh,
        in_specs=placed,
        out_specs=(P(None, "shard", None), P("rep", None, "shard", None), P()),
        check_vma=False,
    )
```

```python
import functools

import jax
import jax.numpy as jnp
from jax import lax
from jax.experimental import pallas as pl
from jax.experimental.pallas import tpu as pltpu
from jax.sharding import PartitionSpec as P

MESH = pl.DeviceIdType.MESH
F32 = jnp.float32
BF16 = jnp.bfloat16
HIGHEST = lax.Precision.HIGHEST

ROWS = 256
KVC = 1024
RANK = 64
NX, NY, NZ = 4, 4, 8
NQ = 2
QR = ROWS // NQ
NCH = 2
KR = RANK // NCH
CPR = NX * NY * 8 // KR
PW = KVC // CPR


def hops(d, n):
    return min(d, n - d)


PLANE = sorted(
    ((dx, dy) for dx in range(NX) for dy in range(NY) if dx or dy),
    key=lambda o: -hops(o[0], NX) - hops(o[1], NY),
)
DIST = [hops(dx, NX) + hops(dy, NY) for dx, dy in PLANE]
ZLINE = sorted(range(1, NZ), key=lambda d: -hops(d, NZ))
YLINE = sorted(range(1, NY), key=lambda d: -hops(d, NY))
FAR = max(DIST)
NP = len(PLANE)


def split(x):
    hi = x.astype(BF16)
    return hi, (x - hi.astype(F32)).astype(BF16)


def nt(a, b, **kw):
    return lax.dot_general(a, b, (((1,), (1,)), ((), ())), preferred_element_type=F32, **kw)


def nn(a, b, **kw):
    return lax.dot_general(a, b, (((1,), (0,)), ((), ())), preferred_element_type=F32, **kw)


def factor_panels(blocks, panels):
    sub_i = lax.broadcasted_iota(jnp.int32, (8, 128), 0)
    for kb in panels:
        live = range(kb, 8)
        cols = {
            b: [jnp.broadcast_to(blocks[b][:, 8 * kb + j : 8 * kb + j + 1], (8, 128)) for j in range(8)]
            for b in live
        }
        for s in range(8):
            row = jnp.broadcast_to(blocks[kb][s : s + 1, :], (8, 128))
            inv = 1.0 / jnp.broadcast_to(cols[kb][s][s : s + 1, :], (8, 128))
            heads = [jnp.broadcast_to(cols[kb][j][s : s + 1, :], (8, 128)) for j in range(8)]
            for b in live:
                f = cols[b][s] * inv
                if b == kb:
                    f = jnp.where(sub_i > s, f, 0.0)
                blocks[b] = blocks[b] - f * row
                for j in range(s + 1, 8):
                    cols[b][j] = cols[b][j] - f * heads[j]
    return blocks


def comm_kernel(
    grad_ref, err_ref, basis_ref,
    rt_out, cinv_out, ot_out, mer,
    g_o, e_o, g_s, e_s, b_v, pin, p_hi, p_lo,
    l1, lr,
    gz_b, gz_r, gx_b, gx_r,
    rs_b, rs_r, z_b, z_r, ag_b, w_b,
    ld, px_s, px_r, l_s, l_r, g_ss, g_rs, rs_s, rs_rs, z_s, z_rs, ag_s, ag_rs, fw_s, fw_r, co_s, co_r,
    near2, near3, near4, near5,
):
    rep, shard = lax.axis_index("rep"), lax.axis_index("shard")
    y, c = rep // 2, rep % 2
    z, x = shard // NX, shard % NX

    def dev(yy, zz, xx, cc=None):
        return (yy * 2 + (c if cc is None else cc), zz * NX + xx)

    partner = dev(y, z, x, 1 - c)
    plane = [(dx, dy, dev((y + dy) % NY, z, (x + dx) % NX, 1)) for dx, dy in PLANE]
    zline = [(d - 1, dev(y, (z + d) % NZ, x)) for d in ZLINE]
    yline = [(d - 1, dev((y + d) % NY, z, x)) for d in YLINE]
    xline = [dev(y, z, (x + d) % NX) for d in range(1, NX)]

    def remote(src, dst, ss, rs, to):
        copy = pltpu.make_async_remote_copy(
            src_ref=src, dst_ref=dst, send_sem=ss, recv_sem=rs, device_id=to, device_id_type=MESH
        )
        copy.start()
        return copy

    def wait_bytes(ref, sem):
        pltpu.make_async_copy(ref, ref, sem).wait()

    oc = 1 - c
    loads = []
    for q in range(NQ):
        rows = pl.ds(q * QR, QR)
        pair = []
        for k, (hbm, buf) in enumerate(((grad_ref, g_o), (err_ref, e_o))):
            cp = pltpu.make_async_copy(hbm.at[oc, rows, :], buf.at[rows, :], ld.at[2 * q + k])
            cp.start()
            pair.append(cp)
        loads.append(pair)
    own_b = pltpu.make_async_copy(basis_ref.at[c], b_v, ld.at[2 * NQ])
    own_b.start()
    own_g = pltpu.make_async_copy(grad_ref.at[c], g_s, ld.at[2 * NQ + 1])
    own_g.start()
    own_e = pltpu.make_async_copy(err_ref.at[c], e_s, ld.at[2 * NQ + 2])
    own_e.start()

    near = [
        dev(y, z, (x + 1) % NX), dev(y, z, (x + NX - 1) % NX),
        dev((y + 1) % NY, z, x), dev((y + NY - 1) % NY, z, x),
        dev(y, (z + 1) % NZ, x), dev(y, (z + NZ - 1) % NZ, x),
    ]

    def tell(sem, peers):
        for d in peers:
            pl.semaphore_signal(sem, inc=1, device_id=d, device_id_type=MESH)

    barrier = pltpu.get_barrier_semaphore()
    tell(barrier, [partner] + near)
    pl.semaphore_wait(barrier, 1 + len(near))
    tell(near2, near)

    px = []
    for q in range(NQ):
        rows = pl.ds(q * QR, QR)
        loads[q][0].wait()
        loads[q][1].wait()
        mer[oc, rows, :] = g_o[rows, :].astype(F32) + e_o[rows, :]
        px.append(remote(mer.at[oc, rows, :], pin.at[rows, :], px_s.at[q], px_r.at[q], partner))
    own_b.wait()
    bt_h, bt_l = split(b_v[...])
    bt2 = jnp.concatenate([bt_h, bt_l], axis=0)
    own_g.wait()
    own_e.wait()
    mer[c] = g_s[...].astype(F32) + e_s[...]
    pl.semaphore_wait(near2, len(near))
    tell(near3, near)
    lq = []
    for q in range(NQ):
        rows = pl.ds(q * QR, QR)
        px[q].wait_recv()
        h, l = split(mer[c, rows, :] + pin[rows, :])
        p_hi[rows, :] = h
        p_lo[rows, :] = l
        t = nt(bt2, h)
        lq.append((t[:RANK] + t[RANK:] + nt(bt_h, l)) * 0.125)
        l1[q] = lq[q]
        for d, to in yline:
            remote(l1.at[q], lr.at[d, q], l_s.at[q], l_r.at[q], to)
        if q == 0:
            pl.semaphore_wait(near3, len(near))
            tell(near4, near)
    pl.semaphore_wait(near4, len(near))
    tell(near5, near)
    for q in range(NQ):
        wait_bytes(lr.at[:, q], l_r.at[q])
        lq[q] = (lq[q] + lr[1, q]) + (lr[0, q] + lr[2, q])
    lt = jnp.concatenate(lq, axis=1)

    def piece(p, j):
        rows = pl.ds(pl.multiple_of(j * KR + (p // CPR) * 8, 8), 8)
        cols = pl.ds(pl.multiple_of((p % CPR) * PW, PW), PW)
        return rows, cols

    me = y * NX + x
    for j in range(NCH):
        rows = slice(j * KR, (j + 1) * KR)
        part = lt[rows]
        h, l = split(part)
        t = nn(jnp.concatenate([h, l], axis=0), p_hi[...])
        rs_b[rows, :] = t[:KR] + t[KR:] + nn(h, p_lo[...])
        if j == 0:
            pl.semaphore_wait(near5, len(near))
        for i, (dx, dy, to) in enumerate(plane):
            at = ((y + dy) % NY) * NX + (x + dx) % NX
            rows, cols = piece(at, j)
            remote(rs_b.at[rows, cols], rs_r.at[c, j, i], rs_s.at[j], rs_rs.at[c, j], to)

        @pl.when(c == 0)
        def _():
            rows, cols = piece(me, j)
            remote(rs_b.at[rows, cols], rs_r.at[0, j, NP], rs_s.at[j], rs_rs.at[0, j], partner)

    gram = nt(lt, lt, precision=HIGHEST)
    gz_b[...] = jnp.concatenate([gram[: RANK // 2], gram[RANK // 2 :]], axis=1)
    for d, to in zline:
        remote(gz_b, gz_r.at[d], g_ss.at[0], g_rs.at[0], to)

    def gram_z():
        wait_bytes(gz_r, g_rs.at[0])
        r = [gz_b[...]] + [gz_r[d] for d in range(NZ - 1)]
        gx_b[...] = ((r[0] + r[4]) + (r[2] + r[6])) + ((r[1] + r[5]) + (r[3] + r[7]))
        for d, to in enumerate(xline):
            remote(gx_b, gx_r.at[d], g_ss.at[1], g_rs.at[1], to)

    def tree(r):
        while len(r) > 1:
            r = [r[i] + r[i + 1] for i in range(0, len(r), 2)]
        return r[0]

    @pl.when(c == 1)
    def _():
        for m in (1, 0):
            for j in range(NCH):
                if m == 1:
                    wait_bytes(rs_r.at[m, j, pl.ds(0, NP)], rs_rs.at[m, j])
                    rows, cols = piece(me, j)
                    last = rs_b[rows, cols]
                else:
                    wait_bytes(rs_r.at[m, j], rs_rs.at[m, j])
                    last = rs_r[m, j, NP]
                total = tree([rs_r[m, j, i] for i in range(NP)] + [last])
                z_b[m, j] = total
                for d in ZLINE:
                    remote(z_b.at[m, j], z_r.at[j, d], z_s.at[m, j], z_rs.at[j], dev(y, (z + d) % NZ, x, 1 - m))
                if m == 0:
                    z_r[j, 0] = total
                else:
                    remote(z_b.at[m, j], z_r.at[j, 0], z_s.at[m, j], z_rs.at[j], partner)

    gram_z()
    for j in range(NCH):

        @pl.when(c == 1)
        def _():
            wait_bytes(z_r.at[j, pl.ds(1, NZ - 1)], z_rs.at[j])

        @pl.when(c == 0)
        def _():
            wait_bytes(z_r.at[j], z_rs.at[j])

        r = [z_r[j, d] for d in range(NZ)]
        total = ((r[0] + r[4]) + (r[2] + r[6])) + ((r[1] + r[5]) + (r[3] + r[7]))
        ag_b[j] = total
        rt_out[oc, j, me] = total
        for i, (dx, dy, to) in enumerate(plane):
            remote(ag_b.at[j], rt_out.at[oc, j, me], ag_s.at[j], ag_rs.at[oc, j, DIST[i] - 1], to)
        remote(ag_b.at[j], rt_out.at[oc, j, me], fw_s.at[0], fw_r.at[0], partner)

    wait_bytes(gx_r, g_rs.at[1])
    g = (gx_b[...] + gx_r[1]) + (gx_r[0] + gx_r[2])
    gram = jnp.concatenate([g[:, :RANK], g[:, RANK:]], axis=0)
    ri = lax.broadcasted_iota(jnp.int32, (RANK, RANK), 0)
    ci = lax.broadcasted_iota(jnp.int32, (RANK, RANK), 1)
    w = jnp.concatenate([gram, jnp.where(ri == ci, 1.0, 0.0)], axis=1)
    blocks = [w[8 * b : 8 * b + 8] for b in range(8)]
    blocks = factor_panels(blocks, range(8))
    w = jnp.concatenate(blocks, axis=0)
    u, low = w[:, :RANK], w[:, RANK:]
    diag = jnp.sum(jnp.where(ri == ci, u, 0.0), axis=1, keepdims=True)
    cinv = low * lax.rsqrt(diag)
    w_b[...] = jnp.concatenate([cinv, jnp.zeros_like(cinv)], axis=1)
    cinv_out[c] = w_b[...]
    ot_out[c] = nn(cinv, lt, precision=HIGHEST)
    remote(cinv_out.at[c], cinv_out.at[c], co_s.at[0], co_r.at[0], partner)
    remote(ot_out.at[c], ot_out.at[c], co_s.at[1], co_r.at[1], partner)
    @pl.when(c == 1)
    def _():
        order = sorted(
            ((m, j, k) for m in range(2) for j in range(NCH) for k in range(FAR)),
            key=lambda t: t[2] * 0.6 + 0.3 * t[1] - 0.4 * t[0],
        )
        for m, j, k in order:
            wait_bytes(rs_r.at[m, j, pl.ds(0, DIST.count(k + 1))], ag_rs.at[m, j, k])
            for (dx, dy), n in zip(PLANE, DIST):
                if n == k + 1:
                    at = ((y + dy) % NY) * NX + (x + dx) % NX
                    remote(rt_out.at[m, j, at], rt_out.at[m, j, at], fw_s.at[1], fw_r.at[1], partner)
        wait_bytes(rt_out.at[:, :, pl.ds(0, NP)], fw_s.at[1])
        for m in range(2):
            for j in range(NCH):
                wait_bytes(z_r.at[j, pl.ds(0, NZ - 1 + m)], z_s.at[m, j])
                wait_bytes(rs_r.at[1, j, pl.ds(0, NP)], rs_s.at[j]) if m else None

    @pl.when(c == 0)
    def _():
        wait_bytes(rt_out.at[:, :, pl.ds(0, NP)], fw_r.at[1])
        for j in range(NCH):
            wait_bytes(rs_r.at[0, j], rs_s.at[j])

    own = rt_out.at[0, :, 0]
    wait_bytes(own, fw_r.at[0])
    wait_bytes(own, fw_s.at[0])
    wait_bytes(cinv_out.at[oc], co_r.at[0])
    wait_bytes(ot_out.at[oc], co_r.at[1])
    for q in range(NQ):
        px[q].wait_send()
    for q in range(NQ):
        wait_bytes(lr.at[:, q], l_s.at[q])
    wait_bytes(gz_r, g_ss.at[0])
    wait_bytes(gx_r, g_ss.at[1])
    for j in range(NCH):
        wait_bytes(rs_r.at[0, j, pl.ds(0, NP)], ag_s.at[j])
    wait_bytes(cinv_out.at[c], co_s.at[0])
    wait_bytes(ot_out.at[c], co_s.at[1])


OB = 64


def out_kernel(mer_ref, rt_ref, cinv_ref, ot_ref, upd_ref, new_ref, next_ref, upd, new, nxt, r3, o3, sems):
    started = []

    def out(src, dst, sem):
        copy = pltpu.make_async_copy(src, dst, sem)
        copy.start()
        started.append(copy)

    for m in range(2):
        ch, cl = split(cinv_ref[m][:, :RANK] * 0.125)
        raw = jnp.concatenate(
            [
                jnp.concatenate([rt_ref[m, j, g * CPR + h] for h in range(CPR)], axis=1)
                for j in range(NCH)
                for g in range(KR // 8)
            ],
            axis=0,
        )
        rh, rl = split(raw)
        right = nn(jnp.concatenate([ch, cl], axis=1), jnp.concatenate([rh, rh], axis=0)) + nn(ch, rl)
        nxt[m] = right
        out(nxt.at[m], next_ref.at[m], sems.at[0, m])
        h, l = split(right)
        r3[m, 0:RANK] = h
        r3[m, RANK : 2 * RANK] = h
        r3[m, 2 * RANK :] = l
        oh, ol = split(ot_ref[m].T)
        o3[m] = jnp.concatenate([oh, ol, oh], axis=1)
    for m in range(2):
        for i in range(ROWS // OB):
            rows = pl.ds(i * OB, OB)
            approx = nn(o3[m, rows, :], r3[m])
            upd[m, rows, :] = approx.astype(BF16)
            new[m, rows, :] = mer_ref[m, rows, :] - approx
            n = m * (ROWS // OB) + i
            out(upd.at[m, rows, :], upd_ref.at[m, rows, :], sems.at[1, n])
            out(new.at[m, rows, :], new_ref.at[m, rows, :], sems.at[2, n])
    for copy in started:
        copy.wait()


def on_device(grad_kv, error_kv, basis_kv):
    grad, err = grad_kv[0], error_kv[0]
    dma = pltpu.SemaphoreType.DMA
    anyspec = pl.BlockSpec(memory_space=pltpu.HBM)
    vspec = pl.BlockSpec(memory_space=pltpu.VMEM)
    rt, cinv, ot, mer = pl.pallas_call(
        comm_kernel,
        name="exchange",
        out_shape=(
            jax.ShapeDtypeStruct((2, NCH, NX * NY, 8, PW), F32),
            jax.ShapeDtypeStruct((2, RANK, 128), F32),
            jax.ShapeDtypeStruct((2, RANK, ROWS), F32),
            jax.ShapeDtypeStruct((2, ROWS, KVC), F32),
        ),
        in_specs=[anyspec] * 3,
        out_specs=(vspec,) * 4,
        scratch_shapes=[
            pltpu.VMEM((ROWS, KVC), BF16),
            pltpu.VMEM((ROWS, KVC), F32),
            pltpu.VMEM((ROWS, KVC), BF16),
            pltpu.VMEM((ROWS, KVC), F32),
            pltpu.VMEM((RANK, KVC), F32),
            pltpu.VMEM((ROWS, KVC), F32),
            pltpu.VMEM((ROWS, KVC), BF16),
            pltpu.VMEM((ROWS, KVC), BF16),
            pltpu.VMEM((NQ, RANK, QR), F32),
            pltpu.VMEM((NY - 1, NQ, RANK, QR), F32),
            pltpu.VMEM((RANK // 2, 128), F32),
            pltpu.VMEM((NZ - 1, RANK // 2, 128), F32),
            pltpu.VMEM((RANK // 2, 128), F32),
            pltpu.VMEM((NX - 1, RANK // 2, 128), F32),
            pltpu.VMEM((RANK, KVC), F32),
            pltpu.VMEM((2, NCH, NP + 1, 8, PW), F32),
            pltpu.VMEM((2, NCH, 8, PW), F32),
            pltpu.VMEM((NCH, NZ, 8, PW), F32),
            pltpu.VMEM((NCH, 8, PW), F32),
            pltpu.VMEM((RANK, 128), F32),
            dma((2 * NQ + 3,)),
            dma((NQ,)),
            dma((NQ,)),
            dma((NQ,)),
            dma((NQ,)),
            dma((2,)),
            dma((2,)),
        ]
        + [dma((NCH,)), dma((2, NCH)), dma((2, NCH)), dma((NCH,)), dma((NCH,)), dma((2, NCH, FAR)), dma((2,)), dma((2,))]
        + [dma((2,)), dma((2,))]
        + [pltpu.SemaphoreType.REGULAR] * 4,
        compiler_params=pltpu.CompilerParams(
            collective_id=0, has_side_effects=True, vmem_limit_bytes=40 << 20
        ),
    )(*(pltpu.with_memory_space_constraint(a, pltpu.HBM) for a in (grad, err, jnp.swapaxes(basis_kv, 1, 2))))
    upd, new, nxt = pl.pallas_call(
        out_kernel,
        name="decompress",
        out_shape=(
            jax.ShapeDtypeStruct((2, ROWS, KVC), BF16),
            jax.ShapeDtypeStruct((2, ROWS, KVC), F32),
            jax.ShapeDtypeStruct((2, RANK, KVC), F32),
        ),
        in_specs=[vspec] * 4,
        out_specs=(anyspec,) * 3,
        scratch_shapes=[
            pltpu.VMEM((2, ROWS, KVC), BF16),
            pltpu.VMEM((2, ROWS, KVC), F32),
            pltpu.VMEM((2, RANK, KVC), F32),
            pltpu.VMEM((2, 3 * RANK, KVC), BF16),
            pltpu.VMEM((2, ROWS, 3 * RANK), BF16),
            dma((3, 2 * ROWS // OB)),
        ],
        compiler_params=pltpu.CompilerParams(vmem_limit_bytes=16 << 20),
    )(mer, rt, cinv, ot)
    return upd, new[None], jnp.swapaxes(nxt, 1, 2)


def solution(mesh):
    placed = (P("rep", None, "shard", None), P("rep", None, "shard", None), P())
    return jax.shard_map(
        on_device,
        mesh=mesh,
        in_specs=placed,
        out_specs=(P(None, "shard", None), P("rep", None, "shard", None), P()),
        check_vma=False,
    )
```
